256 devices in a mesh: island: 8 (over y, x_lo), fsdp: 32 (over z, x_hi, core).
Axes of the slice: x: 4 (x_hi: 2, x_lo: 2; x = x_hi * 2 + x_lo), y: 4, z: 8, core: 2. Of those that a mesh axis runs over, the one named last changes fastest.
Arguments:
- tokens: bfloat16 [65536, 4096], P(('island', 'fsdp')), may hold values from -6 to 6
- upstream: bfloat16 [65536, 1024], P(('island', 'fsdp')), may hold values from -6 to 6
- params: float32 [4096, 1024], P('fsdp'), may hold values from -6 to 6
- momentum: float32 [4096, 1024], P('fsdp'), may hold values from -4 to 4
- projection: float32 [1024, 512], replicated, may hold values from -6 to 6
Outputs:
- values: bfloat16 [65536, 1024], P(('island', 'fsdp'))
- token_grads: bfloat16 [65536, 4096], P(('island', 'fsdp'))
- new_params: float32 [4096, 1024], P('fsdp')
- new_momentum: float32 [4096, 1024], P('fsdp')
The draws below stay inside these ranges and needn't reach their ends.
All inputs are finite; a program needn't handle non-finite values.
Results may differ from the reference program's by a relative error of at most 0.012.
Values may be sent and summed in bfloat16 or wider, within the bound.
No kernel may reach another device: no remote copies, remote signals or barrier semaphores. Data moves between devices by JAX's collectives and lax.ppermute only.
A program may use at most 128 MiB of HBM per device.

```python
import math
import jax
import jax.numpy as jnp
from jax import lax

D = 4096
KV = 1024
PROJ = 512
TOK_ISL = 8192
TOK_ALL = 65536
N_ISLAND = 8


def steps_of(stream_key, dims, cuts, least, largest):
    gain, own = 1.0, jax.random.fold_in(stream_key, 6)
    for position, parts in cuts:
        heights = jnp.exp(jax.random.uniform(jax.random.fold_in(own, position), (parts,), jnp.float32, least / len(cuts), largest / len(cuts)))
        gain = gain * jnp.repeat(heights, dims[position] // parts).reshape([-1 if axis == position else 1 for axis in range(len(dims))])
    return gain


def gaussian(key, shape, width, reach, cuts=(), dtype=jnp.bfloat16):
    entries = jax.random.normal(key, shape, jnp.float32) * width
    if len(cuts) > 0:
        entries = steps_of(key, shape, cuts, -0.22, 0.18) * entries
    return jnp.clip(entries, min=-reach, max=reach).astype(dtype)


def setup_inputs(seed: int = 0) -> dict:
    seeds = jax.random.split(jax.random.key(seed), 6)
    tokens = gaussian(seeds[0], (TOK_ALL, D), 1.0, 6.0, ((0, 256),))
    upstream = gaussian(seeds[1], (TOK_ALL, KV), 1.0, 6.0, ((0, 256),))
    params = gaussian(seeds[2], (D, KV), 1.0, 6.0, ((0, 32),), jnp.float32)
    momentum = gaussian(seeds[3], (D, KV), 0.5, 4.0, ((0, 32),), jnp.float32)
    projection = gaussian(seeds[4], (KV, PROJ), 1.0, 6.0, (), jnp.float32)
    return dict(tokens=tokens, upstream=upstream, params=params, momentum=momentum, projection=projection)


def reference(tokens, upstream, params, momentum, projection):
    half_weight = params.astype(jnp.bfloat16)
    inv_width = 1.0 / math.sqrt(D)
    forward_sum = jnp.dot(tokens, half_weight, preferred_element_type=jnp.float32)
    values = (forward_sum * inv_width).astype(jnp.bfloat16)
    backward_sum = lax.dot_general(upstream, half_weight, (((1,), (1,)), ((), ())), preferred_element_type=jnp.float32)
    token_grads = (backward_sum * inv_width).astype(jnp.bfloat16)
    summed = lax.dot_general(tokens, upstream, (((0,), (0,)), ((), ())), preferred_element_type=jnp.float32)
    pseudo = summed * (1.0 / math.sqrt(TOK_ISL))
    compressed = jnp.dot(pseudo, projection, precision=lax.Precision.HIGHEST)
    outer = jnp.dot(compressed, projection.T, precision=lax.Precision.HIGHEST) / (PROJ * N_ISLAND)
    new_momentum = 0.9 * momentum + outer
    new_params = params - 0.7 * (outer + 0.9 * new_momentum)
    return (values, token_grads, new_params, new_momentum)
```

```python
import functools
import math

import jax
import jax.numpy as jnp
from jax import lax
from jax.experimental import pallas as pl
from jax.experimental.pallas import tpu as pltpu
from jax.sharding import Mesh
from jax.sharding import PartitionSpec as P

ISLAND = ("y", "xl")
FSDP = ("z", "xh", "c")
PLANE = ("y", "xl", "xh")
F32, BF16 = jnp.float32, jnp.bfloat16
LANES = 128


def two_parts(x):
    head = x.astype(BF16)
    return head, (x - head.astype(F32)).astype(BF16)


def pick_kernel(c_ref, tokens_ref, params_ref, out_ref, half_ref):
    skip = 1 - c_ref[0]
    half_ref[...] = params_ref[...].astype(BF16)
    for k in range(out_ref.shape[1] // LANES):
        at = pl.multiple_of((2 * k + skip) * LANES, LANES)
        out_ref[:, k * LANES : (k + 1) * LANES] = tokens_ref[:, pl.ds(at, LANES)]


def pick(c, tokens, params):
    t, d = tokens.shape
    vm = pl.BlockSpec(memory_space=pltpu.VMEM)
    return pl.pallas_call(
        pick_kernel,
        out_shape=(
            jax.ShapeDtypeStruct((t, d // 2), BF16),
            jax.ShapeDtypeStruct(params.shape, BF16),
        ),
        in_specs=[pl.BlockSpec(memory_space=pltpu.SMEM), vm, vm],
        out_specs=(vm, vm),
        name="pick",
    )(c, tokens, params)


def q_kernel(up_ref, proj_ref, q_ref):
    head, rest = two_parts(proj_ref[...])
    q = jnp.dot(up_ref[...], head, preferred_element_type=F32)
    q += jnp.dot(up_ref[...], rest, preferred_element_type=F32)
    q_ref[...] = q.astype(BF16)


def make_q(upstream, projection):
    vm = pl.BlockSpec(memory_space=pltpu.VMEM)
    return pl.pallas_call(
        q_kernel,
        out_shape=jax.ShapeDtypeStruct((upstream.shape[0], projection.shape[1]), BF16),
        in_specs=[vm, vm],
        out_specs=vm,
        name="make_q",
    )(upstream, projection)


def sketch_kernel(c_ref, tok_ref, got_ref, q_ref, got_q_ref, out_ref):
    pieces, n_xh, _, part, proj = out_ref.shape
    z = pl.program_id(0)
    dims = (((0,), (0,)), ((), ()))
    for h in range(n_xh):
        k = z * n_xh + h
        mine = tok_ref[:, pl.ds(pl.multiple_of((2 * k + c_ref[0]) * LANES, LANES), LANES)]
        theirs = got_ref[:, pl.ds(pl.multiple_of(k * LANES, LANES), LANES)]
        s = lax.dot_general(mine, q_ref[...], dims, preferred_element_type=F32)
        s += lax.dot_general(theirs, got_q_ref[...], dims, preferred_element_type=F32)
        out_ref[:, h, 0] = s.astype(BF16).reshape(pieces, part, proj)


def make_sketch(c, tokens, got, q, got_q, pieces, n_xh, n_z):
    t, d = tokens.shape
    proj = q.shape[1]
    part = LANES // pieces
    vm = pl.BlockSpec(memory_space=pltpu.VMEM)
    return pl.pallas_call(
        sketch_kernel,
        grid=(n_z,),
        out_shape=jax.ShapeDtypeStruct((pieces, n_xh, n_z, part, proj), BF16),
        in_specs=[pl.BlockSpec(memory_space=pltpu.SMEM), vm, vm, vm, vm],
        out_specs=pl.BlockSpec((pieces, n_xh, 1, part, proj), lambda z: (0, 0, z, 0, 0)),
        name="make_sketch",
    )(c, tokens, got, q, got_q)


def local(tokens, upstream, params, momentum, projection):
    rows, feat = params.shape
    n_z, n_xh, n_c = (lax.axis_size(a) for a in FSDP)
    n_isl = lax.axis_size("y") * lax.axis_size("xl")
    fsdp_count = n_z * n_xh * n_c
    width = tokens.shape[1]
    proj = projection.shape[1]
    part = rows // n_isl
    inv_width = 1.0 / math.sqrt(width)
    scale_tok = 1.0 / math.sqrt(tokens.shape[0] * fsdp_count)
    c = lax.axis_index("c").astype(jnp.int32).reshape(1)
    swap = functools.partial(lax.ppermute, axis_name="c", perm=[(0, 1), (1, 0)])

    other, half = pick(c, tokens, params)
    got = swap(other)
    weight = lax.all_gather(half, FSDP, axis=0, tiled=True)

    q = make_q(upstream, projection)
    got_q = swap(q)
    pair = make_sketch(c, tokens, got, q, got_q, n_isl, n_xh, n_z)
    pair = pair.reshape(n_isl * n_xh, n_z * part, proj)
    pair = lax.all_to_all(pair, PLANE, 0, 0, tiled=True)
    plane = jnp.sum(pair.astype(F32), axis=0).astype(BF16)
    plane = lax.all_to_all(plane.reshape(n_z, part, proj), "z", 0, 0, tiled=True)
    total = jnp.sum(plane.astype(F32), axis=0).astype(BF16)
    total = jnp.broadcast_to(total[None], (n_isl, part, proj))
    total = lax.all_to_all(total, ISLAND, 0, 0, tiled=True).reshape(rows, proj)

    dims = (((1,), (1,)), ((), ()))
    head, rest = two_parts(projection)
    outer = lax.dot_general(total, head, dims, preferred_element_type=F32)
    outer = outer + lax.dot_general(total, rest, dims, preferred_element_type=F32)
    outer = outer * (scale_tok / (proj * n_isl))
    new_momentum = 0.9 * momentum + outer
    new_params = params - 0.7 * (outer + 0.9 * new_momentum)

    forward_sum = jnp.dot(tokens, weight, preferred_element_type=F32)
    values = (forward_sum * inv_width).astype(BF16)
    product = lax.dot_general(upstream, weight, dims, preferred_element_type=F32)
    token_grads = (product * inv_width).astype(BF16)
    return (values, token_grads, new_params, new_momentum)


def solution(mesh):
    fine = Mesh(mesh.devices.reshape(4, 2, 8, 2, 2), ISLAND + FSDP)
    both = ISLAND + FSDP
    in_specs = (P(both, None), P(both, None), P(FSDP, None), P(FSDP, None), P())
    out_specs = (P(both, None), P(both, None), P(FSDP, None), P(FSDP, None))
    return jax.shard_map(local, mesh=fine, in_specs=in_specs, out_specs=out_specs, check_vma=False)
```

```python
import functools
import math

import jax
import jax.numpy as jnp
from jax import lax
from jax.experimental import pallas as pl
from jax.experimental.pallas import tpu as pltpu
from jax.sharding import Mesh
from jax.sharding import PartitionSpec as P

ISLAND = ("y", "xl")
FSDP = ("z", "xh", "c")
PLANE = ("y", "xl", "xh")
F32, BF16 = jnp.float32, jnp.bfloat16
LANES = 128


def two_parts(x):
    head = x.astype(BF16)
    return head, (x - head.astype(F32)).astype(BF16)


def pick_kernel(at_ref, tokens_ref, params_ref, out_ref, piece_ref):
    skip = 1 - at_ref[0]
    width = piece_ref.shape[2]
    piece = params_ref[:, pl.ds(pl.multiple_of(at_ref[1] * width, width), width)].astype(BF16)
    for z in range(piece_ref.shape[0]):
        piece_ref[z] = piece
    for k in range(out_ref.shape[1] // LANES):
        at = pl.multiple_of((2 * k + skip) * LANES, LANES)
        out_ref[:, k * LANES : (k + 1) * LANES] = tokens_ref[:, pl.ds(at, LANES)]


def pick(at, tokens, params, n_z, n_y):
    t, d = tokens.shape
    rows, kv = params.shape
    vm = pl.BlockSpec(memory_space=pltpu.VMEM)
    return pl.pallas_call(
        pick_kernel,
        out_shape=(
            jax.ShapeDtypeStruct((t, d // 2), BF16),
            jax.ShapeDtypeStruct((n_z, rows, kv // n_y), BF16),
        ),
        in_specs=[pl.BlockSpec(memory_space=pltpu.SMEM), vm, vm],
        out_specs=(vm, vm),
        name="pick",
    )(at, tokens, params)


def q_kernel(up_ref, proj_ref, q_ref):
    head, rest = two_parts(proj_ref[...])
    q = jnp.dot(up_ref[...], head, preferred_element_type=F32)
    q += jnp.dot(up_ref[...], rest, preferred_element_type=F32)
    q_ref[...] = q.astype(BF16)


def make_q(upstream, projection):
    vm = pl.BlockSpec(memory_space=pltpu.VMEM)
    return pl.pallas_call(
        q_kernel,
        out_shape=jax.ShapeDtypeStruct((upstream.shape[0], projection.shape[1]), BF16),
        in_specs=[vm, vm],
        out_specs=vm,
        cost_estimate=pl.CostEstimate(flops=8 * upstream.size * projection.shape[1], bytes_accessed=4 * projection.size + 4 * upstream.size, transcendentals=0),
        name="make_q",
    )(upstream, projection)


def sketch_kernel(at_ref, tok_ref, got_ref, q_ref, got_q_ref, out_ref):
    pieces, n_xh, _, part, proj = out_ref.shape
    z = pl.program_id(0)
    dims = (((0,), (0,)), ((), ()))
    for h in range(n_xh):
        k = z * n_xh + h
        mine = tok_ref[:, pl.ds(pl.multiple_of((2 * k + at_ref[0]) * LANES, LANES), LANES)]
        theirs = got_ref[:, pl.ds(pl.multiple_of(k * LANES, LANES), LANES)]
        s = lax.dot_general(mine, q_ref[...], dims, preferred_element_type=F32)
        s += lax.dot_general(theirs, got_q_ref[...], dims, preferred_element_type=F32)
        out_ref[:, h, 0] = s.astype(BF16).reshape(pieces, part, proj)


def make_sketch(at, tokens, got, q, got_q, pieces, n_xh, n_z):
    t, d = tokens.shape
    proj = q.shape[1]
    part = LANES // pieces
    vm = pl.BlockSpec(memory_space=pltpu.VMEM)
    return pl.pallas_call(
        sketch_kernel,
        grid=(n_z,),
        out_shape=jax.ShapeDtypeStruct((pieces, n_xh, n_z, part, proj), BF16),
        in_specs=[pl.BlockSpec(memory_space=pltpu.SMEM), vm, vm, vm, vm],
        out_specs=pl.BlockSpec((pieces, n_xh, 1, part, proj), lambda z: (0, 0, z, 0, 0)),
        cost_estimate=pl.CostEstimate(flops=8 * tokens.size * proj, bytes_accessed=16 * tokens.size, transcendentals=0),
        name="make_sketch",
    )(at, tokens, got, q, got_q)


GROUPS = (((0, 1, 2), "XAB"), ((3, 4, 5), "ABX"), ((6, 7), "BXA"))
FLIP = {"X": (1, 0), "A": (0, 1), "B": (0, 3)}


def exchange(x, kind):
    if kind == "X":
        return lax.ppermute(x, ("xl", "xh"), [(0, 3), (3, 0), (1, 2), (2, 1)])
    flip = FLIP[kind][1]
    return lax.ppermute(x, "y", [(i, i ^ flip) for i in range(4)])


def places():
    table = {}
    for g, (zs, order) in enumerate(GROUPS):
        held = [(0, 0)]
        for step, kind in enumerate(order):
            there = [(a ^ FLIP[kind][0], b ^ FLIP[kind][1]) for a, b in held]
            if step == 2:
                for half, part in enumerate((held, there)):
                    for i, (a, b) in enumerate(part):
                        for k, z in enumerate(zs):
                            table[z, a, b] = (g, half, i * len(zs) + k)
            held = held + there
    return table


def product_kernel(at_ref, tok_ref, up_ref, *refs, scale):
    w_refs, (values_ref, grads_ref, acc_ref, up_rel) = refs[:-4], refs[-4:]
    c, y, xh = at_ref[0], at_ref[1], at_ref[2]
    n_y = 4
    width = up_ref.shape[1] // n_y
    table = places()
    cols = [pl.ds(pl.multiple_of((y ^ b) * width, width), width) for b in range(n_y)]
    for b in range(n_y):
        up_rel[:, b * width : (b + 1) * width] = up_ref[:, cols[b]]
    acc_ref[...] = jnp.zeros(acc_ref.shape, F32)
    for z in range(8):
        for a in range(2):
            shard = 2 * (2 * z + (xh ^ a))
            blocks = [pl.ds(pl.multiple_of((shard + (c ^ o)) * LANES, LANES), LANES) for o in range(2)]
            w = []
            for o in range(2):
                row = []
                for b in range(n_y):
                    g, half, i = table[z, a, b]
                    row.append(w_refs[4 * g + 2 * o + half][i])
                w.append(jnp.concatenate(row, axis=1))
            w = jnp.concatenate(w, axis=0)
            toks = jnp.concatenate([tok_ref[:, at] for at in blocks], axis=1)
            acc_ref[...] += jnp.dot(toks, w, preferred_element_type=F32)
            grad = lax.dot_general(up_rel[...], w, (((1,), (1,)), ((), ())), preferred_element_type=F32)
            grad = (grad * scale).astype(BF16)
            for o in range(2):
                grads_ref[:, blocks[o]] = grad[:, o * LANES : (o + 1) * LANES]
    for b in range(n_y):
        values_ref[:, cols[b]] = (acc_ref[:, b * width : (b + 1) * width] * scale).astype(BF16)


def products(at, tokens, upstream, weights, scale):
    t, d = tokens.shape
    kv = upstream.shape[1]
    vm = pl.BlockSpec(memory_space=pltpu.VMEM)
    return pl.pallas_call(
        functools.partial(product_kernel, scale=scale),
        out_shape=(jax.ShapeDtypeStruct((t, kv), BF16), jax.ShapeDtypeStruct((t, d), BF16)),
        in_specs=[pl.BlockSpec(memory_space=pltpu.SMEM)] + [vm] * (2 + len(weights)),
        out_specs=(vm, vm),
        scratch_shapes=[pltpu.VMEM((t, kv), F32), pltpu.VMEM((t, kv), BF16)],
        cost_estimate=pl.CostEstimate(
            flops=4 * t * d * kv, bytes_accessed=2 * d * kv + 4 * t * (d + kv), transcendentals=0
        ),
        name="products",
    )(at, tokens, upstream, *weights)


def local(tokens, upstream, params, momentum, projection):
    rows, feat = params.shape
    n_z, n_xh, n_c = (lax.axis_size(a) for a in FSDP)
    n_isl = lax.axis_size("y") * lax.axis_size("xl")
    fsdp_count = n_z * n_xh * n_c
    width = tokens.shape[1]
    proj = projection.shape[1]
    part = rows // n_isl
    inv_width = 1.0 / math.sqrt(width)
    scale_tok = 1.0 / math.sqrt(tokens.shape[0] * fsdp_count)
    at = jnp.stack([lax.axis_index(a).astype(jnp.int32) for a in ("c", "y", "xh")])
    swap = functools.partial(lax.ppermute, axis_name="c", perm=[(0, 1), (1, 0)])

    other, piece = pick(at, tokens, params, n_z, lax.axis_size("y"))
    got = swap(other)
    piece = lax.all_to_all(piece, "z", 0, 0, tiled=True)

    q = make_q(upstream, projection)
    got_q = swap(q)
    pair = make_sketch(at, tokens, got, q, got_q, n_isl, n_xh, n_z)
    held = [piece[zs[0] : zs[-1] + 1] for zs, _ in GROUPS]
    for step in range(2):
        more = [exchange(h, order[step]) for h, (_, order) in zip(held, GROUPS)]
        held = [jnp.concatenate(pair_, axis=0) for pair_ in zip(held, more)]
    last = [exchange(h, order[2]) for h, (_, order) in zip(held, GROUPS)]
    weights = []
    for near, far in zip(held, last):
        weights += [near, far, swap(near), swap(far)]

    pair = pair.reshape(n_isl * n_xh, n_z * part, proj)
    pair = lax.all_to_all(pair, PLANE, 0, 0, tiled=True)
    plane = jnp.sum(pair.astype(F32), axis=0).astype(BF16)
    plane = lax.all_to_all(plane.reshape(n_z, part, proj), "z", 0, 0, tiled=True)
    total = jnp.sum(plane.astype(F32), axis=0).astype(BF16)
    total = jnp.broadcast_to(total[None], (n_isl, part, proj))
    total = lax.all_to_all(total, ISLAND, 0, 0, tiled=True).reshape(rows, proj)

    dims = (((1,), (1,)), ((), ()))
    head, rest = two_parts(projection)
    outer = lax.dot_general(total, head, dims, preferred_element_type=F32)
    outer = outer + lax.dot_general(total, rest, dims, preferred_element_type=F32)
    outer = outer * (scale_tok / (proj * n_isl))
    new_momentum = 0.9 * momentum + outer
    new_params = params - 0.7 * (outer + 0.9 * new_momentum)

    values, token_grads = products(at, tokens, upstream, weights, inv_width)
    return (values, token_grads, new_params, new_momentum)


def solution(mesh):
    fine = Mesh(mesh.devices.reshape(4, 2, 8, 2, 2), ISLAND + FSDP)
    both = ISLAND + FSDP
    in_specs = (P(both, None), P(both, None), P(FSDP, None), P(FSDP, None), P())
    out_specs = (P(both, None), P(both, None), P(FSDP, None), P(FSDP, None))
    return jax.shard_map(local, mesh=fine, in_specs=in_specs, out_specs=out_specs, check_vma=False)
```

```python
import functools
import math

import jax
import jax.numpy as jnp
from jax import lax
from jax.experimental import pallas as pl
from jax.experimental.pallas import tpu as pltpu
from jax.sharding import Mesh
from jax.sharding import PartitionSpec as P


ISLAND = ("y", "xl")
FSDP = ("z", "xh", "c")
PLANE = ("y", "xl", "xh")
F32, BF16 = jnp.float32, jnp.bfloat16
LANES = 128
VMEM = pl.BlockSpec(memory_space=pltpu.VMEM)
SMEM = pl.BlockSpec(memory_space=pltpu.SMEM)
LEFT = pl.BlockSpec(memory_space=pl.ANY)


def two_parts(x):
    head = x.astype(BF16)
    return head, (x - head.astype(F32)).astype(BF16)


def pick_kernel(at_ref, tokens_ref, params_ref, out_ref, piece_ref):
    skip = 1 - at_ref[0]
    width = piece_ref.shape[2]
    block = 2 * at_ref[1] + at_ref[3]
    piece = params_ref[:, pl.ds(pl.multiple_of(block * width, width), width)].astype(BF16)
    for z in range(piece_ref.shape[0]):
        piece_ref[z] = piece
    for k in range(out_ref.shape[1] // LANES):
        at = pl.multiple_of((2 * k + skip) * LANES, LANES)
        out_ref[:, k * LANES : (k + 1) * LANES] = tokens_ref[:, pl.ds(at, LANES)]


def pick(at, tokens, params, n_z, pieces):
    t, d = tokens.shape
    rows, kv = params.shape
    return pl.pallas_call(
        pick_kernel,
        out_shape=(
            jax.ShapeDtypeStruct((t, d // 2), BF16),
            jax.ShapeDtypeStruct((n_z, rows, kv // pieces), BF16),
        ),
        in_specs=[SMEM, VMEM, VMEM],
        out_specs=(VMEM, VMEM),
        name="pick",
    )(at, tokens, params)


def q_kernel(up_ref, proj_ref, q_ref):
    head, rest = two_parts(proj_ref[...])
    q = jnp.dot(up_ref[...], head, preferred_element_type=F32)
    q += jnp.dot(up_ref[...], rest, preferred_element_type=F32)
    q_ref[...] = q.astype(BF16)


def make_q(upstream, projection):
    vm = pl.BlockSpec(memory_space=pltpu.VMEM)
    return pl.pallas_call(
        q_kernel,
        out_shape=jax.ShapeDtypeStruct((upstream.shape[0], projection.shape[1]), BF16),
        in_specs=[vm, vm],
        out_specs=vm,
        cost_estimate=pl.CostEstimate(flops=8 * upstream.size * projection.shape[1], bytes_accessed=4 * projection.size + 4 * upstream.size, transcendentals=0),
        name="make_q",
    )(upstream, projection)


def sketch_kernel(at_ref, tok_ref, got_ref, q_ref, got_q_ref, out_ref):
    pieces, n_xh, _, part, proj = out_ref.shape
    z = pl.program_id(0)
    dims = (((0,), (0,)), ((), ()))
    for h in range(n_xh):
        k = z * n_xh + h
        mine = tok_ref[:, pl.ds(pl.multiple_of((2 * k + at_ref[0]) * LANES, LANES), LANES)]
        theirs = got_ref[:, pl.ds(pl.multiple_of(k * LANES, LANES), LANES)]
        s = lax.dot_general(mine, q_ref[...], dims, preferred_element_type=F32)
        s += lax.dot_general(theirs, got_q_ref[...], dims, preferred_element_type=F32)
        out_ref[:, h, 0] = s.astype(BF16).reshape(pieces, part, proj)


def make_sketch(at, tokens, got, q, got_q, pieces, n_xh, n_z):
    proj = q.shape[1]
    part = LANES // pieces
    vm = pl.BlockSpec(memory_space=pltpu.VMEM)
    return pl.pallas_call(
        sketch_kernel,
        grid=(n_z,),
        out_shape=jax.ShapeDtypeStruct((pieces, n_xh, n_z, part, proj), BF16),
        in_specs=[pl.BlockSpec(memory_space=pltpu.SMEM), vm, vm, vm, vm],
        out_specs=pl.BlockSpec((pieces, n_xh, 1, part, proj), lambda z: (0, 0, z, 0, 0)),
        cost_estimate=pl.CostEstimate(flops=8 * tokens.size * proj, bytes_accessed=16 * tokens.size, transcendentals=0),
        name="make_sketch",
    )(at, tokens, got, q, got_q)


GROUPS = ("XALB", "ALBX", "LBXA", "BXAL")
FLIP = {"X": (1, 0, 1), "L": (0, 0, 1), "A": (0, 1, 0), "B": (0, 3, 0)}


def exchange(x, kind):
    if kind == "X":
        return lax.ppermute(x, ("xl", "xh"), [(0, 3), (3, 0), (1, 2), (2, 1)])
    if kind == "L":
        return lax.ppermute(x, "xl", [(0, 1), (1, 0)])
    flip = FLIP[kind][1]
    return lax.ppermute(x, "y", [(i, i ^ flip) for i in range(4)])


def places(n_z):
    table = {}
    each = n_z // len(GROUPS)
    for g, order in enumerate(GROUPS):
        held = [(0, 0, 0)]
        for step, kind in enumerate(order):
            f = FLIP[kind]
            there = [(a ^ f[0], b ^ f[1], l ^ f[2]) for a, b, l in held]
            if step == 3:
                for half, part in enumerate((held, there)):
                    for k in range(each):
                        for a in range(2):
                            table[half, g * each + k, a] = sorted(
                                ((b, l), g, i * each + k) for i, (a_, b, l) in enumerate(part) if a_ == a
                            )
            held = held + there
    return table


def split_kernel(piece_ref, after_ref, *out_refs):
    each = out_refs[0].shape[0]
    for g, out_ref in enumerate(out_refs):
        out_ref[...] = piece_ref[g * each : (g + 1) * each]


def split(piece, after):
    n = len(GROUPS)
    shape = (piece.shape[0] // n,) + piece.shape[1:]
    return pl.pallas_call(
        split_kernel,
        out_shape=(jax.ShapeDtypeStruct(shape, BF16),) * n,
        in_specs=[VMEM, LEFT],
        out_specs=(VMEM,) * n,
        name="split",
    )(piece, after)


def join_kernel(after_ref, *refs):
    n = len(refs) // 3
    for a_ref, b_ref, out_ref in zip(refs[:n], refs[n : 2 * n], refs[2 * n :]):
        k = a_ref.shape[0]
        out_ref[:k] = a_ref[...]
        out_ref[k:] = b_ref[...]


def join(held, more, after):
    n = len(held)
    shapes = tuple(jax.ShapeDtypeStruct((2 * h.shape[0],) + h.shape[1:], BF16) for h in held)
    return pl.pallas_call(
        join_kernel, out_shape=shapes, in_specs=[LEFT] + [VMEM] * (2 * n), out_specs=(VMEM,) * n, name="join"
    )(after, *held, *more)


def lanes(ref, blocks):
    return jnp.concatenate([ref[:, at] for at in blocks], axis=1)


def half_products(half, at_ref, tok_ref, up_ref, w_refs, acc_ref, up_rel, take):
    c, y, xh, xl = (at_ref[i] for i in range(4))
    n = len(GROUPS)
    n_z = tok_ref.shape[1] // (4 * LANES)
    table = places(n_z)
    cols = [
        pl.ds(pl.multiple_of((2 * (y ^ (r // 2)) + (xl ^ (r % 2))) * LANES, LANES), LANES) for r in range(8)
    ]
    for r in range(8):
        up_rel[:, r * LANES : (r + 1) * LANES] = up_ref[:, cols[r]]
    for z in range(n_z):
        for a in range(2):
            shard = 2 * (2 * z + (xh ^ a))
            blocks = [pl.ds(pl.multiple_of((shard + (c ^ o)) * LANES, LANES), LANES) for o in range(2)]
            found = table[half, z, a]
            total = None
            if found:
                w = jnp.concatenate(
                    [
                        jnp.concatenate([w_refs[n * o + g][i] for _, g, i in found], axis=1)
                        for o in range(2)
                    ],
                    axis=0,
                )
                here = [slice((2 * b + l) * LANES, (2 * b + l + 1) * LANES) for (b, l), _, _ in found]
                part = jnp.dot(lanes(tok_ref, blocks), w, preferred_element_type=F32)
                for i, at in enumerate(here):
                    acc_ref[:, at] += part[:, i * LANES : (i + 1) * LANES]
                total = lax.dot_general(
                    lanes(up_rel, here), w, (((1,), (1,)), ((), ())), preferred_element_type=F32
                )
            take(z, a, blocks, total)
    return cols


def near_kernel(at_ref, tok_ref, up_ref, *refs):
    w_refs, (acc_ref, sum_ref, up_rel) = refs[:-3], refs[-3:]
    acc_ref[...] = jnp.zeros(acc_ref.shape, F32)

    def take(z, a, blocks, total):
        if total is not None:
            sum_ref[2 * z + a] = total

    half_products(0, at_ref, tok_ref, up_ref, w_refs, acc_ref, up_rel, take)


def far_kernel(at_ref, tok_ref, up_ref, before_ref, sum_ref, *refs, scale):
    w_refs, (values_ref, grads_ref, acc_ref, up_rel) = refs[:-4], refs[-4:]
    acc_ref[...] = before_ref[...]
    near = places(tok_ref.shape[1] // (4 * LANES))

    def take(z, a, blocks, total):
        if near[0, z, a]:
            total = sum_ref[2 * z + a] if total is None else total + sum_ref[2 * z + a]
        grad = (total * scale).astype(BF16)
        for o in range(2):
            grads_ref[:, blocks[o]] = grad[:, o * LANES : (o + 1) * LANES]

    cols = half_products(1, at_ref, tok_ref, up_ref, w_refs, acc_ref, up_rel, take)
    for r in range(8):
        values_ref[:, cols[r]] = (acc_ref[:, r * LANES : (r + 1) * LANES] * scale).astype(BF16)


def near_products(at, tokens, upstream, weights):
    t, d = tokens.shape
    kv = upstream.shape[1]
    return pl.pallas_call(
        near_kernel,
        out_shape=(
            jax.ShapeDtypeStruct((t, kv), F32),
            jax.ShapeDtypeStruct((d // (2 * LANES), t, 2 * LANES), F32),
        ),
        in_specs=[SMEM] + [VMEM] * (2 + len(weights)),
        out_specs=(VMEM, VMEM),
        scratch_shapes=[pltpu.VMEM((t, kv), BF16)],
        cost_estimate=pl.CostEstimate(flops=2 * t * d * kv, bytes_accessed=d * kv, transcendentals=0),
        name="near_products",
    )(at, tokens, upstream, *weights)


def far_products(at, tokens, upstream, acc, sums, weights, scale):
    t, d = tokens.shape
    kv = upstream.shape[1]
    return pl.pallas_call(
        functools.partial(far_kernel, scale=scale),
        out_shape=(jax.ShapeDtypeStruct((t, kv), BF16), jax.ShapeDtypeStruct((t, d), BF16)),
        in_specs=[SMEM] + [VMEM] * (4 + len(weights)),
        out_specs=(VMEM, VMEM),
        scratch_shapes=[pltpu.VMEM((t, kv), F32), pltpu.VMEM((t, kv), BF16)],
        cost_estimate=pl.CostEstimate(flops=2 * t * d * kv, bytes_accessed=d * kv, transcendentals=0),
        name="far_products",
    )(at, tokens, upstream, acc, sums, *weights)


def step(tokens, upstream, params, momentum, projection):
    rows, _ = params.shape
    n_z, n_xh, n_c = (lax.axis_size(a) for a in FSDP)
    n_isl = lax.axis_size("y") * lax.axis_size("xl")
    fsdp_count = n_z * n_xh * n_c
    width = tokens.shape[1]
    proj = projection.shape[1]
    part = rows // n_isl
    inv_width = 1.0 / math.sqrt(width)
    scale_tok = 1.0 / math.sqrt(tokens.shape[0] * fsdp_count)
    at = jnp.stack([lax.axis_index(a).astype(jnp.int32) for a in ("c", "y", "xh", "xl")])
    swap = functools.partial(lax.ppermute, axis_name="c", perm=[(0, 1), (1, 0)])

    other, piece = pick(at, tokens, params, n_z, n_isl)
    got = swap(other)
    piece = lax.all_to_all(piece, "z", 0, 0, tiled=True)

    q = make_q(upstream, projection)
    got_q = swap(q)
    pair = make_sketch(at, tokens, got, q, got_q, n_isl, n_xh, n_z)
    held = split(piece, pair)
    held = join(held, [exchange(h, order[0]) for h, order in zip(held, GROUPS)], pair)
    more = [exchange(h, order[1]) for h, order in zip(held, GROUPS)]
    pair = pair.reshape(n_isl * n_xh, n_z * part, proj)
    pair = lax.all_to_all(pair, PLANE, 0, 0, tiled=True)
    plane = jnp.sum(pair.astype(F32), axis=0).astype(BF16)
    held = join(held, more, plane)
    more = [exchange(h, order[2]) for h, order in zip(held, GROUPS)]
    plane = lax.all_to_all(plane.reshape(n_z, part, proj), "z", 0, 0, tiled=True)
    total = jnp.sum(plane.astype(F32), axis=0).astype(BF16)
    held = join(held, more, total)
    far = [exchange(h, order[3]) for h, order in zip(held, GROUPS)]
    total = jnp.broadcast_to(total[None], (n_isl, part, proj))
    total = lax.all_to_all(total, ISLAND, 0, 0, tiled=True).reshape(rows, proj)

    held = [*held, *(swap(h) for h in held)]
    acc, sums = near_products(at, tokens, upstream, held)
    far = [*far, *(swap(f) for f in far)]
    values, token_grads = far_products(at, tokens, upstream, acc, sums, far, inv_width)

    dims = (((1,), (1,)), ((), ()))
    head, rest = two_parts(projection)
    outer = lax.dot_general(total, head, dims, preferred_element_type=F32)
    outer = outer + lax.dot_general(total, rest, dims, preferred_element_type=F32)
    outer = outer * (scale_tok / (proj * n_isl))
    new_momentum = 0.9 * momentum + outer
    new_params = params - 0.7 * (outer + 0.9 * new_momentum)

    return (values, token_grads, new_params, new_momentum)


def solution(mesh):
    fine = Mesh(mesh.devices.reshape(4, 2, 8, 2, 2), ISLAND + FSDP)
    both = ISLAND + FSDP
    in_specs = (P(both, None), P(both, None), P(FSDP, None), P(FSDP, None), P())
    out_specs = (P(both, None), P(both, None), P(FSDP, None), P(FSDP, None))
    return jax.shard_map(step, mesh=fine, in_specs=in_specs, out_specs=out_specs, check_vma=False)
```

```python
import functools
import math

import jax
import jax.numpy as jnp
from jax import lax
from jax.experimental import pallas as pl
from jax.experimental.pallas import tpu as pltpu
from jax.sharding import Mesh
from jax.sharding import PartitionSpec as P


ISLAND = ("y", "xl")
FSDP = ("z", "xh", "c")
PLANE = ("y", "xl", "xh")
F32, BF16 = jnp.float32, jnp.bfloat16
LANES = 128
VMEM = pl.BlockSpec(memory_space=pltpu.VMEM)
SMEM = pl.BlockSpec(memory_space=pltpu.SMEM)


def two_parts(x):
    head = x.astype(BF16)
    return head, (x - head.astype(F32)).astype(BF16)


def pick_kernel(c_ref, tokens_ref, params_ref, out_ref, half_ref):
    skip = 1 - c_ref[0]
    half_ref[...] = params_ref[...].astype(BF16)
    for k in range(out_ref.shape[1] // LANES):
        at = pl.multiple_of((2 * k + skip) * LANES, LANES)
        out_ref[:, k * LANES : (k + 1) * LANES] = tokens_ref[:, pl.ds(at, LANES)]


def pick(c, tokens, params):
    t, d = tokens.shape
    vm = pl.BlockSpec(memory_space=pltpu.VMEM)
    return pl.pallas_call(
        pick_kernel,
        out_shape=(
            jax.ShapeDtypeStruct((t, d // 2), BF16),
            jax.ShapeDtypeStruct(params.shape, BF16),
        ),
        in_specs=[pl.BlockSpec(memory_space=pltpu.SMEM), vm, vm],
        out_specs=(vm, vm),
        name="pick",
    )(c, tokens, params)


def q_kernel(up_ref, proj_ref, q_ref):
    head, rest = two_parts(proj_ref[...])
    q = jnp.dot(up_ref[...], head, preferred_element_type=F32)
    q += jnp.dot(up_ref[...], rest, preferred_element_type=F32)
    q_ref[...] = q.astype(BF16)


def make_q(upstream, projection):
    vm = pl.BlockSpec(memory_space=pltpu.VMEM)
    return pl.pallas_call(
        q_kernel,
        out_shape=jax.ShapeDtypeStruct((upstream.shape[0], projection.shape[1]), BF16),
        in_specs=[vm, vm],
        out_specs=vm,
        cost_estimate=pl.CostEstimate(flops=8 * upstream.size * projection.shape[1], bytes_accessed=4 * projection.size + 4 * upstream.size, transcendentals=0),
        name="make_q",
    )(upstream, projection)


def sketch_kernel(c_ref, tok_ref, got_ref, q_ref, got_q_ref, out_ref):
    pieces, n_xh, _, part, proj = out_ref.shape
    z = pl.program_id(0)
    dims = (((0,), (0,)), ((), ()))
    for h in range(n_xh):
        k = z * n_xh + h
        mine = tok_ref[:, pl.ds(pl.multiple_of((2 * k + c_ref[0]) * LANES, LANES), LANES)]
        theirs = got_ref[:, pl.ds(pl.multiple_of(k * LANES, LANES), LANES)]
        s = lax.dot_general(mine, q_ref[...], dims, preferred_element_type=F32)
        s += lax.dot_general(theirs, got_q_ref[...], dims, preferred_element_type=F32)
        out_ref[:, h, 0] = s.astype(BF16).reshape(pieces, part, proj)


def make_sketch(c, tokens, got, q, got_q, pieces, n_xh, n_z):
    proj = q.shape[1]
    part = LANES // pieces
    vm = pl.BlockSpec(memory_space=pltpu.VMEM)
    return pl.pallas_call(
        sketch_kernel,
        grid=(n_z,),
        out_shape=jax.ShapeDtypeStruct((pieces, n_xh, n_z, part, proj), BF16),
        in_specs=[pl.BlockSpec(memory_space=pltpu.SMEM), vm, vm, vm, vm],
        out_specs=pl.BlockSpec((pieces, n_xh, 1, part, proj), lambda z: (0, 0, z, 0, 0)),
        cost_estimate=pl.CostEstimate(flops=8 * tokens.size * proj, bytes_accessed=16 * tokens.size, transcendentals=0),
        name="make_sketch",
    )(c, tokens, got, q, got_q)


def share_kernel(at_ref, tok_ref, up_ref, w_ref, acc_ref, grads_ref, *, scale, packed):
    n = w_ref.shape[0] // LANES
    acc = jnp.zeros(acc_ref.shape, F32)
    step = 4
    for k in range(0, n, step):
        if packed:
            toks = tok_ref[:, k * LANES : (k + step) * LANES]
        else:
            at = [pl.multiple_of((2 * j + at_ref[0]) * LANES, LANES) for j in range(k, k + step)]
            toks = jnp.concatenate([tok_ref[:, pl.ds(a, LANES)] for a in at], axis=1)
        w = w_ref[k * LANES : (k + step) * LANES]
        acc += jnp.dot(toks, w, preferred_element_type=F32)
        g = lax.dot_general(up_ref[...], w, (((1,), (1,)), ((), ())), preferred_element_type=F32)
        grads_ref[:, k * LANES : (k + step) * LANES] = (g * scale).astype(BF16)
    acc_ref[...] = acc


def share(at, tokens, upstream, weight, scale, packed):
    t, kv = upstream.shape
    rows = weight.shape[0]
    return pl.pallas_call(
        functools.partial(share_kernel, scale=scale, packed=packed),
        out_shape=(jax.ShapeDtypeStruct((t, kv), F32), jax.ShapeDtypeStruct((t, rows), BF16)),
        in_specs=[SMEM, VMEM, VMEM, VMEM],
        out_specs=(VMEM, VMEM),
        cost_estimate=pl.CostEstimate(
            flops=4 * t * rows * kv, bytes_accessed=2 * rows * kv + 4 * t * rows, transcendentals=0
        ),
        name="their_share" if packed else "my_share",
    )(at, tokens, upstream, weight)


def meet_kernel(at_ref, acc_ref, got_acc_ref, grads_ref, got_ref, values_ref, out_ref, *, scale):
    values_ref[...] = ((acc_ref[...] + got_acc_ref[...]) * scale).astype(BF16)
    for k in range(grads_ref.shape[1] // LANES):
        here = slice(k * LANES, (k + 1) * LANES)
        mine = pl.ds(pl.multiple_of((2 * k + at_ref[0]) * LANES, LANES), LANES)
        theirs = pl.ds(pl.multiple_of((2 * k + 1 - at_ref[0]) * LANES, LANES), LANES)
        out_ref[:, mine] = grads_ref[:, here]
        out_ref[:, theirs] = got_ref[:, here]


def meet(at, acc, got_acc, grads, got, scale):
    t, kv = acc.shape
    return pl.pallas_call(
        functools.partial(meet_kernel, scale=scale),
        out_shape=(jax.ShapeDtypeStruct((t, kv), BF16), jax.ShapeDtypeStruct((t, 2 * grads.shape[1]), BF16)),
        in_specs=[SMEM] + [VMEM] * 4,
        out_specs=(VMEM, VMEM),
        name="meet",
    )(at, acc, got_acc, grads, got)


def step(tokens, upstream, params, momentum, projection):
    rows, _ = params.shape
    n_z, n_xh, n_c = (lax.axis_size(a) for a in FSDP)
    n_isl = lax.axis_size("y") * lax.axis_size("xl")
    fsdp_count = n_z * n_xh * n_c
    width = tokens.shape[1]
    proj = projection.shape[1]
    part = rows // n_isl
    inv_width = 1.0 / math.sqrt(width)
    scale_tok = 1.0 / math.sqrt(tokens.shape[0] * fsdp_count)
    c = lax.axis_index("c").astype(jnp.int32).reshape(1)
    swap = functools.partial(lax.ppermute, axis_name="c", perm=[(0, 1), (1, 0)])

    other, half = pick(c, tokens, params)
    got = swap(other)
    own = lax.all_gather(half, FSDP[:2], axis=0, tiled=True)
    got_up = swap(upstream)

    q = make_q(upstream, projection)
    got_q = swap(q)
    pair = make_sketch(c, tokens, got, q, got_q, n_isl, n_xh, n_z)
    pair = pair.reshape(n_isl * n_xh, n_z * part, proj)
    pair = lax.all_to_all(pair, PLANE, 0, 0, tiled=True)
    plane = jnp.sum(pair.astype(F32), axis=0).astype(BF16)
    plane = lax.all_to_all(plane.reshape(n_z, part, proj), "z", 0, 0, tiled=True)
    total = jnp.sum(plane.astype(F32), axis=0).astype(BF16)
    total = jnp.broadcast_to(total[None], (n_isl, part, proj))
    total = lax.all_to_all(total, ISLAND, 0, 0, tiled=True).reshape(rows, proj)

    dims = (((1,), (1,)), ((), ()))
    head, rest = two_parts(projection)
    outer = lax.dot_general(total, head, dims, preferred_element_type=F32)
    outer = outer + lax.dot_general(total, rest, dims, preferred_element_type=F32)
    outer = outer * (scale_tok / (proj * n_isl))
    new_momentum = 0.9 * momentum + outer
    new_params = params - 0.7 * (outer + 0.9 * new_momentum)

    their_acc, their_grads = share(c, got, got_up, own, inv_width, True)
    got_acc, got_grads = swap(their_acc), swap(their_grads)
    acc, grads = share(c, tokens, upstream, own, inv_width, False)
    values, token_grads = meet(c, acc, got_acc, grads, got_grads, inv_width)
    return (values, token_grads, new_params, new_momentum)


def solution(mesh):
    fine = Mesh(mesh.devices.reshape(4, 2, 8, 2, 2), ISLAND + FSDP)
    both = ISLAND + FSDP
    in_specs = (P(both, None), P(both, None), P(FSDP, None), P(FSDP, None), P())
    out_specs = (P(both, None), P(both, None), P(FSDP, None), P(FSDP, None))
    return jax.shard_map(step, mesh=fine, in_specs=in_specs, out_specs=out_specs, check_vma=False)
```

```python
import functools
import math

import jax
import jax.numpy as jnp
from jax import lax
from jax.experimental import pallas as pl
from jax.experimental.pallas import tpu as pltpu
from jax.sharding import Mesh
from jax.sharding import PartitionSpec as P


ISLAND = ("y", "xl")
FSDP = ("z", "xh", "c")
PLANE = ("xh", "y", "xl")
F32, BF16 = jnp.float32, jnp.bfloat16
LANES = 128
VMEM = pl.BlockSpec(memory_space=pltpu.VMEM)
SMEM = pl.BlockSpec(memory_space=pltpu.SMEM)
LEFT = pl.BlockSpec(memory_space=pl.ANY)


def two_parts(x):
    head = x.astype(BF16)
    return head, (x - head.astype(F32)).astype(BF16)


def pick_kernel(at_ref, tokens_ref, params_ref, out_ref, piece_ref):
    skip = 1 - at_ref[0]
    width = piece_ref.shape[2]
    piece = params_ref[:, pl.ds(pl.multiple_of(at_ref[1] * width, width), width)].astype(BF16)
    for z in range(piece_ref.shape[0]):
        piece_ref[z] = piece
    for k in range(out_ref.shape[1] // LANES):
        at = pl.multiple_of((2 * k + skip) * LANES, LANES)
        out_ref[:, k * LANES : (k + 1) * LANES] = tokens_ref[:, pl.ds(at, LANES)]


def pick(at, tokens, params, n_z, pieces):
    t, d = tokens.shape
    rows, kv = params.shape
    return pl.pallas_call(
        pick_kernel,
        out_shape=(
            jax.ShapeDtypeStruct((t, d // 2), BF16),
            jax.ShapeDtypeStruct((n_z, rows, kv // pieces), BF16),
        ),
        in_specs=[SMEM, VMEM, VMEM],
        out_specs=(VMEM, VMEM),
        name="pick",
    )(at, tokens, params)


def q_kernel(up_ref, proj_ref, q_ref):
    head, rest = two_parts(proj_ref[...])
    q = jnp.dot(up_ref[...], head, preferred_element_type=F32)
    q += jnp.dot(up_ref[...], rest, preferred_element_type=F32)
    q_ref[...] = q.astype(BF16)


def make_q(upstream, projection):
    vm = pl.BlockSpec(memory_space=pltpu.VMEM)
    return pl.pallas_call(
        q_kernel,
        out_shape=jax.ShapeDtypeStruct((upstream.shape[0], projection.shape[1]), BF16),
        in_specs=[vm, vm],
        out_specs=vm,
        cost_estimate=pl.CostEstimate(flops=8 * upstream.size * projection.shape[1], bytes_accessed=4 * projection.size + 4 * upstream.size, transcendentals=0),
        name="make_q",
    )(upstream, projection)


def sketch_kernel(at_ref, tok_ref, got_ref, q_ref, got_q_ref, after_ref, *out_refs):
    n_z = len(out_refs)
    n_xh = out_refs[0].shape[0]
    dims = (((0,), (0,)), ((), ()))
    for r, out_ref in enumerate(out_refs):
        z = lax.rem(at_ref[2] + r, n_z)
        for h in range(n_xh):
            k = z * n_xh + h
            mine = tok_ref[:, pl.ds(pl.multiple_of((2 * k + at_ref[0]) * LANES, LANES), LANES)]
            theirs = got_ref[:, pl.ds(pl.multiple_of(k * LANES, LANES), LANES)]
            s = lax.dot_general(mine, q_ref[...], dims, preferred_element_type=F32)
            s += lax.dot_general(theirs, got_q_ref[...], dims, preferred_element_type=F32)
            out_ref[h] = s.astype(BF16)


def make_sketch(at, tokens, got, q, got_q, n_z, n_xh, after):
    proj = q.shape[1]
    return pl.pallas_call(
        sketch_kernel,
        out_shape=(jax.ShapeDtypeStruct((n_xh, LANES, proj), BF16),) * n_z,
        in_specs=[SMEM] + [VMEM] * 4 + [LEFT],
        out_specs=(VMEM,) * n_z,
        cost_estimate=pl.CostEstimate(
            flops=8 * tokens.size * proj, bytes_accessed=16 * tokens.size, transcendentals=0
        ),
        name="make_sketch",
    )(at, tokens, got, q, got_q, after)


def spread_kernel(piece_ref, *refs):
    out_ref = refs[-1]
    out_ref[0] = piece_ref[...]


def spread(piece, n, *after):
    shape = piece.shape
    return pl.pallas_call(
        spread_kernel,
        grid=(n,),
        out_shape=jax.ShapeDtypeStruct((n,) + shape, BF16),
        in_specs=[VMEM] + [LEFT] * len(after),
        out_specs=pl.BlockSpec((1,) + shape, lambda i: (i, 0, 0, 0)),
        name="spread",
    )(piece, *after)


def share_kernel(at_ref, tok_ref, up_ref, w_ref, acc_ref, grads_ref, *, scale, packed):
    pieces = acc_ref.shape[1] // w_ref.shape[3]
    n_xh = w_ref.shape[0] // pieces
    n = n_xh * w_ref.shape[1]
    acc = jnp.zeros(acc_ref.shape, F32)
    step = 4
    for k in range(0, n, step):
        if packed:
            toks = tok_ref[:, k * LANES : (k + step) * LANES]
        else:
            at = [pl.multiple_of((2 * j + at_ref[0]) * LANES, LANES) for j in range(k, k + step)]
            toks = jnp.concatenate([tok_ref[:, pl.ds(a, LANES)] for a in at], axis=1)
        rows = []
        for j in range(k, k + step):
            z, h = j // n_xh, j % n_xh
            rows.append(jnp.concatenate([w_ref[h * pieces + p, z] for p in range(pieces)], axis=1))
        w = jnp.concatenate(rows, axis=0)
        acc += jnp.dot(toks, w, preferred_element_type=F32)
        g = lax.dot_general(up_ref[...], w, (((1,), (1,)), ((), ())), preferred_element_type=F32)
        grads_ref[:, k * LANES : (k + step) * LANES] = (g * scale).astype(BF16)
    acc_ref[...] = acc


def share(at, tokens, upstream, weight, scale, packed):
    t, kv = upstream.shape
    rows = weight.size // kv
    return pl.pallas_call(
        functools.partial(share_kernel, scale=scale, packed=packed),
        out_shape=(jax.ShapeDtypeStruct((t, kv), F32), jax.ShapeDtypeStruct((t, rows), BF16)),
        in_specs=[SMEM, VMEM, VMEM, VMEM],
        out_specs=(VMEM, VMEM),
        cost_estimate=pl.CostEstimate(
            flops=4 * t * rows * kv, bytes_accessed=2 * rows * kv + 4 * t * rows, transcendentals=0
        ),
        name="their_share" if packed else "my_share",
    )(at, tokens, upstream, weight)


def meet_kernel(at_ref, acc_ref, got_acc_ref, grads_ref, got_ref, values_ref, out_ref, *, scale):
    values_ref[...] = ((acc_ref[...] + got_acc_ref[...]) * scale).astype(BF16)
    for k in range(grads_ref.shape[1] // LANES):
        here = slice(k * LANES, (k + 1) * LANES)
        mine = pl.ds(pl.multiple_of((2 * k + at_ref[0]) * LANES, LANES), LANES)
        theirs = pl.ds(pl.multiple_of((2 * k + 1 - at_ref[0]) * LANES, LANES), LANES)
        out_ref[:, mine] = grads_ref[:, here]
        out_ref[:, theirs] = got_ref[:, here]


def meet(at, acc, got_acc, grads, got, scale):
    t, kv = acc.shape
    return pl.pallas_call(
        functools.partial(meet_kernel, scale=scale),
        out_shape=(jax.ShapeDtypeStruct((t, kv), BF16), jax.ShapeDtypeStruct((t, 2 * grads.shape[1]), BF16)),
        in_specs=[SMEM] + [VMEM] * 4,
        out_specs=(VMEM, VMEM),
        name="meet",
    )(at, acc, got_acc, grads, got)


def step(tokens, upstream, params, momentum, projection):
    rows, _ = params.shape
    n_z, n_xh, n_c = (lax.axis_size(a) for a in FSDP)
    n_isl = lax.axis_size("y") * lax.axis_size("xl")
    fsdp_count = n_z * n_xh * n_c
    width = tokens.shape[1]
    proj = projection.shape[1]
    part = rows // n_isl
    inv_width = 1.0 / math.sqrt(width)
    scale_tok = 1.0 / math.sqrt(tokens.shape[0] * fsdp_count)
    at = jnp.stack([lax.axis_index("c"), lax.axis_index(ISLAND), lax.axis_index("z")]).astype(jnp.int32)
    swap = functools.partial(lax.ppermute, axis_name="c", perm=[(0, 1), (1, 0)])

    other, piece = pick(at, tokens, params, n_z, n_isl)
    got = swap(other)
    piece = lax.all_to_all(piece, "z", 0, 0, tiled=True)
    q = make_q(upstream, projection)
    got_q = swap(q)
    got_up = swap(upstream)

    wide = spread(piece, n_xh * n_isl, got, got_q)
    own = lax.all_to_all(wide, PLANE, 0, 0, tiled=True)

    pair = make_sketch(at, tokens, got, q, got_q, n_z, n_xh, wide)
    along = pair[0].astype(F32)
    for k in sorted(range(1, n_z), key=lambda k: -min(k, n_z - k)):
        shift = [(i, (i + k) % n_z) for i in range(n_z)]
        came = lax.ppermute(pair[k], "z", shift)
        along += came.astype(F32)
    along = along.astype(BF16)
    plane = lax.all_to_all(along.reshape(n_xh * n_isl, part, proj), PLANE, 0, 0, tiled=True)
    total = jnp.sum(plane.astype(F32), axis=0).astype(BF16)
    total = jnp.broadcast_to(total[None], (n_isl, part, proj))
    total = lax.all_to_all(total, ISLAND, 0, 0, tiled=True).reshape(rows, proj)

    dims = (((1,), (1,)), ((), ()))
    head, rest = two_parts(projection)
    outer = lax.dot_general(total, head, dims, preferred_element_type=F32)
    outer = outer + lax.dot_general(total, rest, dims, preferred_element_type=F32)
    outer = outer * (scale_tok / (proj * n_isl))
    new_momentum = 0.9 * momentum + outer
    new_params = params - 0.7 * (outer + 0.9 * new_momentum)

    their_acc, their_grads = share(at, got, got_up, own, inv_width, True)
    got_acc, got_grads = swap(their_acc), swap(their_grads)
    acc, grads = share(at, tokens, upstream, own, inv_width, False)
    values, token_grads = meet(at, acc, got_acc, grads, got_grads, inv_width)
    return (values, token_grads, new_params, new_momentum)


def solution(mesh):
    fine = Mesh(mesh.devices.reshape(4, 2, 8, 2, 2), ISLAND + FSDP)
    both = ISLAND + FSDP
    in_specs = (P(both, None), P(both, None), P(FSDP, None), P(FSDP, None), P())
    out_specs = (P(both, None), P(both, None), P(FSDP, None), P(FSDP, None))
    return jax.shard_map(step, mesh=fine, in_specs=in_specs, out_specs=out_specs, check_vma=False)
```

```python
import functools
import math

import jax
import jax.numpy as jnp
from jax import lax
from jax.experimental import pallas as pl
from jax.experimental.pallas import tpu as pltpu
from jax.sharding import Mesh
from jax.sharding import PartitionSpec as P


ISLAND = ("y", "xl")
FSDP = ("z", "xh", "c")
PLANE = ("xh", "y", "xl")
F32, BF16 = jnp.float32, jnp.bfloat16
LANES = 128
VMEM = pl.BlockSpec(memory_space=pltpu.VMEM)
SMEM = pl.BlockSpec(memory_space=pltpu.SMEM)
LEFT = pl.BlockSpec(memory_space=pl.ANY)


def two_parts(x):
    head = x.astype(BF16)
    return head, (x - head.astype(F32)).astype(BF16)


def pick_kernel(at_ref, tokens_ref, params_ref, out_ref, piece_ref):
    skip = 1 - at_ref[0]
    width = piece_ref.shape[2]
    block = 2 * at_ref[1] + at_ref[3]
    piece = params_ref[:, pl.ds(pl.multiple_of(block * width, width), width)].astype(BF16)
    for z in range(piece_ref.shape[0]):
        piece_ref[z] = piece
    for k in range(out_ref.shape[1] // LANES):
        at = pl.multiple_of((2 * k + skip) * LANES, LANES)
        out_ref[:, k * LANES : (k + 1) * LANES] = tokens_ref[:, pl.ds(at, LANES)]


def pick(at, tokens, params, n_z, pieces):
    t, d = tokens.shape
    rows, kv = params.shape
    return pl.pallas_call(
        pick_kernel,
        out_shape=(
            jax.ShapeDtypeStruct((t, d // 2), BF16),
            jax.ShapeDtypeStruct((n_z, rows, kv // pieces), BF16),
        ),
        in_specs=[SMEM, VMEM, VMEM],
        out_specs=(VMEM, VMEM),
        name="pick",
    )(at, tokens, params)


def q_kernel(up_ref, proj_ref, q_ref):
    head, rest = two_parts(proj_ref[...])
    q = jnp.dot(up_ref[...], head, preferred_element_type=F32)
    q += jnp.dot(up_ref[...], rest, preferred_element_type=F32)
    q_ref[...] = q.astype(BF16)


def make_q(upstream, projection):
    vm = pl.BlockSpec(memory_space=pltpu.VMEM)
    return pl.pallas_call(
        q_kernel,
        out_shape=jax.ShapeDtypeStruct((upstream.shape[0], projection.shape[1]), BF16),
        in_specs=[vm, vm],
        out_specs=vm,
        cost_estimate=pl.CostEstimate(flops=8 * upstream.size * projection.shape[1], bytes_accessed=4 * projection.size + 4 * upstream.size, transcendentals=0),
        name="make_q",
    )(upstream, projection)


def sketch_kernel(at_ref, tok_ref, got_ref, q_ref, got_q_ref, out_ref):
    n_z, n_xh = out_ref.shape[:2]
    dims = (((0,), (0,)), ((), ()))
    for k in range(n_z * n_xh):
        mine = tok_ref[:, pl.ds(pl.multiple_of((2 * k + at_ref[0]) * LANES, LANES), LANES)]
        theirs = got_ref[:, k * LANES : (k + 1) * LANES]
        s = lax.dot_general(mine, q_ref[...], dims, preferred_element_type=F32)
        s += lax.dot_general(theirs, got_q_ref[...], dims, preferred_element_type=F32)
        out_ref[k // n_xh, k % n_xh] = s.astype(BF16)


def make_sketch(at, tokens, got, q, got_q, n_z, n_xh):
    proj = q.shape[1]
    return pl.pallas_call(
        sketch_kernel,
        out_shape=jax.ShapeDtypeStruct((n_z, n_xh, LANES, proj), BF16),
        in_specs=[SMEM] + [VMEM] * 4,
        out_specs=VMEM,
        cost_estimate=pl.CostEstimate(
            flops=8 * tokens.size * proj, bytes_accessed=16 * tokens.size, transcendentals=0
        ),
        name="make_sketch",
    )(at, tokens, got, q, got_q)


GROUPS = ("XALB", "ALBX", "LBXA", "BXAL")
FLIP = {"X": (1, 0, 1), "L": (0, 0, 1), "A": (0, 1, 0), "B": (0, 3, 0)}


def exchange(x, kind):
    if kind == "X":
        return lax.ppermute(x, ("xl", "xh"), [(0, 3), (3, 0), (1, 2), (2, 1)])
    if kind == "L":
        return lax.ppermute(x, "xl", [(0, 1), (1, 0)])
    flip = FLIP[kind][1]
    return lax.ppermute(x, "y", [(i, i ^ flip) for i in range(4)])


def places(n_z):
    table = {}
    each = n_z // len(GROUPS)
    for g, order in enumerate(GROUPS):
        held = [(0, 0, 0)]
        for step, kind in enumerate(order):
            f = FLIP[kind]
            there = [(a ^ f[0], b ^ f[1], l ^ f[2]) for a, b, l in held]
            if step == 3:
                for half, part in enumerate((held, there)):
                    for k in range(each):
                        for a in range(2):
                            table[half, g * each + k, a] = sorted(
                                ((b, l), g, i * each + k) for i, (a_, b, l) in enumerate(part) if a_ == a
                            )
            held = held + there
    return table


def split_kernel(piece_ref, after_ref, *out_refs):
    each = out_refs[0].shape[0]
    for g, out_ref in enumerate(out_refs):
        out_ref[...] = piece_ref[g * each : (g + 1) * each]


def split(piece, after):
    n = len(GROUPS)
    shape = (piece.shape[0] // n,) + piece.shape[1:]
    return pl.pallas_call(
        split_kernel,
        out_shape=(jax.ShapeDtypeStruct(shape, BF16),) * n,
        in_specs=[VMEM, LEFT],
        out_specs=(VMEM,) * n,
        name="split",
    )(piece, after)


def join_kernel(*refs):
    n = len(refs) // 3
    for a_ref, b_ref, out_ref in zip(refs[:n], refs[n : 2 * n], refs[2 * n :]):
        k = a_ref.shape[0]
        out_ref[:k] = a_ref[...]
        out_ref[k:] = b_ref[...]


def join(held, more):
    n = len(held)
    shapes = tuple(jax.ShapeDtypeStruct((2 * h.shape[0],) + h.shape[1:], BF16) for h in held)
    return pl.pallas_call(
        join_kernel, out_shape=shapes, in_specs=[VMEM] * (2 * n), out_specs=(VMEM,) * n, name="join"
    )(*held, *more)


def lanes(ref, blocks):
    return jnp.concatenate([ref[:, at] for at in blocks], axis=1)


def half_products(half, at_ref, tok_ref, up_ref, w_refs, acc_ref, up_rel, take):
    c, y, xh, xl = (at_ref[i] for i in range(4))
    n = len(GROUPS)
    n_z = tok_ref.shape[1] // (4 * LANES)
    table = places(n_z)
    cols = [
        pl.ds(pl.multiple_of((2 * (y ^ (r // 2)) + (xl ^ (r % 2))) * LANES, LANES), LANES) for r in range(8)
    ]
    for r in range(8):
        up_rel[:, r * LANES : (r + 1) * LANES] = up_ref[:, cols[r]]
    for z in range(n_z):
        for a in range(2):
            shard = 2 * (2 * z + (xh ^ a))
            blocks = [pl.ds(pl.multiple_of((shard + (c ^ o)) * LANES, LANES), LANES) for o in range(2)]
            found = table[half, z, a]
            total = None
            if found:
                w = jnp.concatenate(
                    [
                        jnp.concatenate([w_refs[n * o + g][i] for _, g, i in found], axis=1)
                        for o in range(2)
                    ],
                    axis=0,
                )
                here = [slice((2 * b + l) * LANES, (2 * b + l + 1) * LANES) for (b, l), _, _ in found]
                part = jnp.dot(lanes(tok_ref, blocks), w, preferred_element_type=F32)
                for i, at in enumerate(here):
                    acc_ref[:, at] += part[:, i * LANES : (i + 1) * LANES]
                total = lax.dot_general(
                    lanes(up_rel, here), w, (((1,), (1,)), ((), ())), preferred_element_type=F32
                )
            take(z, a, blocks, total)
    return cols


def near_kernel(at_ref, tok_ref, up_ref, *refs):
    w_refs, (acc_ref, sum_ref, up_rel) = refs[:-3], refs[-3:]
    acc_ref[...] = jnp.zeros(acc_ref.shape, F32)

    def take(z, a, blocks, total):
        if total is not None:
            sum_ref[2 * z + a] = total

    half_products(0, at_ref, tok_ref, up_ref, w_refs, acc_ref, up_rel, take)


def far_kernel(at_ref, tok_ref, up_ref, before_ref, sum_ref, *refs, scale):
    w_refs, (values_ref, grads_ref, acc_ref, up_rel) = refs[:-4], refs[-4:]
    acc_ref[...] = before_ref[...]
    near = places(tok_ref.shape[1] // (4 * LANES))

    def take(z, a, blocks, total):
        if near[0, z, a]:
            total = sum_ref[2 * z + a] if total is None else total + sum_ref[2 * z + a]
        grad = (total * scale).astype(BF16)
        for o in range(2):
            grads_ref[:, blocks[o]] = grad[:, o * LANES : (o + 1) * LANES]

    cols = half_products(1, at_ref, tok_ref, up_ref, w_refs, acc_ref, up_rel, take)
    for r in range(8):
        values_ref[:, cols[r]] = (acc_ref[:, r * LANES : (r + 1) * LANES] * scale).astype(BF16)


def near_products(at, tokens, upstream, weights):
    t, d = tokens.shape
    kv = upstream.shape[1]
    return pl.pallas_call(
        near_kernel,
        out_shape=(
            jax.ShapeDtypeStruct((t, kv), F32),
            jax.ShapeDtypeStruct((d // (2 * LANES), t, 2 * LANES), F32),
        ),
        in_specs=[SMEM] + [VMEM] * (2 + len(weights)),
        out_specs=(VMEM, VMEM),
        scratch_shapes=[pltpu.VMEM((t, kv), BF16)],
        cost_estimate=pl.CostEstimate(flops=2 * t * d * kv, bytes_accessed=d * kv, transcendentals=0),
        name="near_products",
    )(at, tokens, upstream, *weights)


def far_products(at, tokens, upstream, acc, sums, weights, scale):
    t, d = tokens.shape
    kv = upstream.shape[1]
    return pl.pallas_call(
        functools.partial(far_kernel, scale=scale),
        out_shape=(jax.ShapeDtypeStruct((t, kv), BF16), jax.ShapeDtypeStruct((t, d), BF16)),
        in_specs=[SMEM] + [VMEM] * (4 + len(weights)),
        out_specs=(VMEM, VMEM),
        scratch_shapes=[pltpu.VMEM((t, kv), F32), pltpu.VMEM((t, kv), BF16)],
        cost_estimate=pl.CostEstimate(flops=2 * t * d * kv, bytes_accessed=d * kv, transcendentals=0),
        name="far_products",
    )(at, tokens, upstream, acc, sums, *weights)


def step(tokens, upstream, params, momentum, projection):
    rows, _ = params.shape
    n_z, n_xh, n_c = (lax.axis_size(a) for a in FSDP)
    n_isl = lax.axis_size("y") * lax.axis_size("xl")
    fsdp_count = n_z * n_xh * n_c
    width = tokens.shape[1]
    proj = projection.shape[1]
    part = rows // n_isl
    inv_width = 1.0 / math.sqrt(width)
    scale_tok = 1.0 / math.sqrt(tokens.shape[0] * fsdp_count)
    at = jnp.stack([lax.axis_index(a).astype(jnp.int32) for a in ("c", "y", "xh", "xl")])
    swap = functools.partial(lax.ppermute, axis_name="c", perm=[(0, 1), (1, 0)])

    other, piece = pick(at, tokens, params, n_z, n_isl)
    got = swap(other)
    piece = lax.all_to_all(piece, "z", 0, 0, tiled=True)

    q = make_q(upstream, projection)
    got_q = swap(q)
    pair = make_sketch(at, tokens, got, q, got_q, n_z, n_xh)
    along = lax.all_to_all(pair, "z", 0, 0, tiled=True)
    held = split(piece, pair)
    for step in range(3):
        held = join(held, [exchange(h, order[step]) for h, order in zip(held, GROUPS)])
    far = [exchange(h, order[3]) for h, order in zip(held, GROUPS)]
    held = [*held, *(swap(h) for h in held)]
    acc, sums = near_products(at, tokens, upstream, held)
    far = [*far, *(swap(f) for f in far)]
    values, token_grads = far_products(at, tokens, upstream, acc, sums, far, inv_width)

    along = jnp.sum(along.astype(F32), axis=0).astype(BF16)
    plane = lax.all_to_all(along.reshape(n_xh * n_isl, part, proj), PLANE, 0, 0, tiled=True)
    total = jnp.sum(plane.astype(F32), axis=0).astype(BF16)
    total = jnp.broadcast_to(total[None], (n_isl, part, proj))
    total = lax.all_to_all(total, ISLAND, 0, 0, tiled=True).reshape(rows, proj)

    dims = (((1,), (1,)), ((), ()))
    head, rest = two_parts(projection)
    outer = lax.dot_general(total, head, dims, preferred_element_type=F32)
    outer = outer + lax.dot_general(total, rest, dims, preferred_element_type=F32)
    outer = outer * (scale_tok / (proj * n_isl))
    new_momentum = 0.9 * momentum + outer
    new_params = params - 0.7 * (outer + 0.9 * new_momentum)

    return (values, token_grads, new_params, new_momentum)


def solution(mesh):
    fine = Mesh(mesh.devices.reshape(4, 2, 8, 2, 2), ISLAND + FSDP)
    both = ISLAND + FSDP
    in_specs = (P(both, None), P(both, None), P(FSDP, None), P(FSDP, None), P())
    out_specs = (P(both, None), P(both, None), P(FSDP, None), P(FSDP, None))
    return jax.shard_map(step, mesh=fine, in_specs=in_specs, out_specs=out_specs, check_vma=False)
```

```python
import functools
import math

import jax
import jax.numpy as jnp
from jax import lax
from jax.experimental import pallas as pl
from jax.experimental.pallas import tpu as pltpu
from jax.sharding import Mesh
from jax.sharding import PartitionSpec as P


ISLAND = ("y", "xl")
FSDP = ("z", "xh", "c")
PLANE = ("xh", "y", "xl")
F32, BF16 = jnp.float32, jnp.bfloat16
LANES = 128
VMEM = pl.BlockSpec(memory_space=pltpu.VMEM)
SMEM = pl.BlockSpec(memory_space=pltpu.SMEM)
LEFT = pl.BlockSpec(memory_space=pl.ANY)


def two_parts(x):
    head = x.astype(BF16)
    return head, (x - head.astype(F32)).astype(BF16)


def piece_kernel(at_ref, params_ref, piece_ref):
    width = piece_ref.shape[2]
    block = 2 * at_ref[1] + at_ref[3]
    piece = params_ref[:, pl.ds(pl.multiple_of(block * width, width), width)].astype(BF16)
    for z in range(piece_ref.shape[0]):
        piece_ref[z] = piece


def make_piece(at, params, n_z, pieces):
    rows, kv = params.shape
    return pl.pallas_call(
        piece_kernel,
        out_shape=jax.ShapeDtypeStruct((n_z, rows, kv // pieces), BF16),
        in_specs=[SMEM, VMEM],
        out_specs=VMEM,
        name="make_piece",
    )(at, params)


def pick_kernel(at_ref, tokens_ref, after_ref, out_ref):
    skip = 1 - at_ref[0]
    for k in range(out_ref.shape[1] // LANES):
        at = pl.multiple_of((2 * k + skip) * LANES, LANES)
        out_ref[:, k * LANES : (k + 1) * LANES] = tokens_ref[:, pl.ds(at, LANES)]


def pick(at, tokens, after):
    t, d = tokens.shape
    return pl.pallas_call(
        pick_kernel,
        out_shape=jax.ShapeDtypeStruct((t, d // 2), BF16),
        in_specs=[SMEM, VMEM, LEFT],
        out_specs=VMEM,
        name="pick",
    )(at, tokens, after)


def q_kernel(up_ref, proj_ref, q_ref):
    head, rest = two_parts(proj_ref[...])
    q = jnp.dot(up_ref[...], head, preferred_element_type=F32)
    q += jnp.dot(up_ref[...], rest, preferred_element_type=F32)
    q_ref[...] = q.astype(BF16)


def make_q(upstream, projection):
    return pl.pallas_call(
        q_kernel,
        out_shape=jax.ShapeDtypeStruct((upstream.shape[0], projection.shape[1]), BF16),
        in_specs=[VMEM, VMEM],
        out_specs=VMEM,
        cost_estimate=pl.CostEstimate(
            flops=8 * upstream.size * projection.shape[1],
            bytes_accessed=4 * projection.size + 4 * upstream.size,
            transcendentals=0,
        ),
        name="make_q",
    )(upstream, projection)


def sketch_kernel(at_ref, tok_ref, got_ref, q_ref, got_q_ref, out_ref):
    n_z, n_xh = out_ref.shape[:2]
    dims = (((0,), (0,)), ((), ()))
    for k in range(n_z * n_xh):
        mine = tok_ref[:, pl.ds(pl.multiple_of((2 * k + at_ref[0]) * LANES, LANES), LANES)]
        theirs = got_ref[:, k * LANES : (k + 1) * LANES]
        s = lax.dot_general(mine, q_ref[...], dims, preferred_element_type=F32)
        s += lax.dot_general(theirs, got_q_ref[...], dims, preferred_element_type=F32)
        out_ref[k // n_xh, k % n_xh] = s.astype(BF16)


def make_sketch(at, tokens, got, q, got_q, n_z, n_xh):
    proj = q.shape[1]
    return pl.pallas_call(
        sketch_kernel,
        out_shape=jax.ShapeDtypeStruct((n_z, n_xh, LANES, proj), BF16),
        in_specs=[SMEM] + [VMEM] * 4,
        out_specs=VMEM,
        cost_estimate=pl.CostEstimate(
            flops=8 * tokens.size * proj, bytes_accessed=16 * tokens.size, transcendentals=0
        ),
        name="make_sketch",
    )(at, tokens, got, q, got_q)


ORDERS = (("XALB", "LBXA"), ("ALBX", "BXAL"))
GROUPS = len(ORDERS[0])
FLIP = {"X": (1, 0, 1), "L": (0, 0, 1), "A": (0, 1, 0), "B": (0, 3, 0)}


def exchange(x, group, step):
    def index(y, xl, xh, c):
        return ((y * 2 + xl) * 2 + xh) * 2 + c

    pairs = []
    for y in range(4):
        for xl in range(2):
            for xh in range(2):
                for c in range(2):
                    a, b, l = FLIP[ORDERS[c][group][step]]
                    pairs.append((index(y, xl, xh, c), index(y ^ b, xl ^ l, xh ^ a, c)))
    return lax.ppermute(x, ("y", "xl", "xh", "c"), pairs)


def places(core, group):
    order = ORDERS[core][group]
    held = [(0, 0, 0)]
    for kind in order[:3]:
        f = FLIP[kind]
        held = held + [(a ^ f[0], b ^ f[1], l ^ f[2]) for a, b, l in held]
    f = FLIP[order[3]]
    far = [(a ^ f[0], b ^ f[1], l ^ f[2]) for a, b, l in held]
    return {
        (half, a): sorted(((b, l), i) for i, (a_, b, l) in enumerate(part) if a_ == a)
        for half, part in enumerate((held, far))
        for a in range(2)
    }


def split_kernel(piece_ref, after_ref, *out_refs):
    each = out_refs[0].shape[0]
    for g, out_ref in enumerate(out_refs):
        out_ref[...] = piece_ref[g * each : (g + 1) * each]


def split(piece, after):
    n = GROUPS
    shape = (piece.shape[0] // n,) + piece.shape[1:]
    return pl.pallas_call(
        split_kernel,
        out_shape=(jax.ShapeDtypeStruct(shape, BF16),) * n,
        in_specs=[VMEM, LEFT],
        out_specs=(VMEM,) * n,
        name="split",
    )(piece, after)


def join_kernel(*refs):
    n = len(refs) // 3
    for a_ref, b_ref, out_ref in zip(refs[:n], refs[n : 2 * n], refs[2 * n :]):
        k = a_ref.shape[0]
        out_ref[:k] = a_ref[...]
        out_ref[k:] = b_ref[...]


def join(held, more):
    n = len(held)
    shapes = tuple(jax.ShapeDtypeStruct((2 * h.shape[0],) + h.shape[1:], BF16) for h in held)
    return pl.pallas_call(
        join_kernel, out_shape=shapes, in_specs=[VMEM] * (2 * n), out_specs=(VMEM,) * n, name="join"
    )(*held, *more)


def lanes(ref, blocks):
    return jnp.concatenate([ref[:, at] for at in blocks], axis=1)


def half_products(half, groups, core, at_ref, tok_ref, w_refs, acc_ref, up_rel, take):
    xh = at_ref[2]
    each = w_refs[0].shape[0] // 8
    for n, g in enumerate(groups):
        for o in range(2):
            table = places(core ^ o, g)
            w_ref = w_refs[len(groups) * o + n]
            for a in range(2):
                zs = range(g * each, (g + 1) * each)
                blocks = [
                    pl.ds(pl.multiple_of((2 * (2 * z + (xh ^ a)) + (core ^ o)) * LANES, LANES), LANES) for z in zs
                ]
                found = table[half, a]
                total = None
                if found:
                    w = jnp.concatenate(
                        [
                            jnp.concatenate([w_ref[i * each + k] for _, i in found], axis=1)
                            for k in range(each)
                        ],
                        axis=0,
                    )
                    here = [slice((2 * b + l) * LANES, (2 * b + l + 1) * LANES) for (b, l), _ in found]
                    part = jnp.dot(lanes(tok_ref, blocks), w, preferred_element_type=F32)
                    for i, at in enumerate(here):
                        acc_ref[:, at] += part[:, i * LANES : (i + 1) * LANES]
                    total = lax.dot_general(
                        lanes(up_rel, here), w, (((1,), (1,)), ((), ())), preferred_element_type=F32
                    )
                take(g, a, o, blocks, total)


def columns(at_ref):
    y, xl = at_ref[1], at_ref[3]
    return [
        pl.ds(pl.multiple_of((2 * (y ^ (r // 2)) + (xl ^ (r % 2))) * LANES, LANES), LANES) for r in range(8)
    ]


def arrange(at_ref, up_ref, up_rel):
    for r, at in enumerate(columns(at_ref)):
        up_rel[:, r * LANES : (r + 1) * LANES] = up_ref[:, at]


def near_kernel(at_ref, tok_ref, up_ref, *refs):
    w_refs, (acc_ref, sum_ref, up_rel) = refs[:-3], refs[-3:]
    acc_ref[...] = jnp.zeros(acc_ref.shape, F32)
    arrange(at_ref, up_ref, up_rel)

    def take(g, a, o, blocks, total):
        if total is not None:
            sum_ref[(2 * g + a) * 2 + o] = total

    for core in range(2):

        @pl.when(at_ref[0] == core)
        def _():
            half_products(0, range(GROUPS), core, at_ref, tok_ref, w_refs, acc_ref, up_rel, take)


def far_kernel(at_ref, tok_ref, up_ref, before_ref, sum_ref, *refs, group, scale, last):
    w_refs = refs[:2]
    if last:
        part_ref, values_ref, grads_ref, acc_ref, up_rel = refs[2:]
        done = part_ref.shape[1]
        grads_ref[:, :done] = part_ref[...]
    else:
        acc_ref, grads_ref, up_rel = refs[2:]
    acc_ref[...] = before_ref[...]
    arrange(at_ref, up_ref, up_rel)

    for core in range(2):

        def take(g, a, o, blocks, total, core=core):
            if places(core ^ o, g)[0, a]:
                before = sum_ref[(2 * g + a) * 2 + o]
                total = before if total is None else total + before
            grad = (total * scale).astype(BF16)
            for k, at in enumerate(blocks):
                grads_ref[:, at] = grad[:, k * LANES : (k + 1) * LANES]

        @pl.when(at_ref[0] == core)
        def _():
            half_products(1, (group,), core, at_ref, tok_ref, w_refs, acc_ref, up_rel, take)

    if last:
        for r, at in enumerate(columns(at_ref)):
            values_ref[:, at] = (acc_ref[:, r * LANES : (r + 1) * LANES] * scale).astype(BF16)


def near_products(at, tokens, upstream, weights):
    t, d = tokens.shape
    kv = upstream.shape[1]
    return pl.pallas_call(
        near_kernel,
        out_shape=(
            jax.ShapeDtypeStruct((t, kv), F32),
            jax.ShapeDtypeStruct((4 * GROUPS, t, d // (4 * GROUPS)), F32),
        ),
        in_specs=[SMEM] + [VMEM] * (2 + len(weights)),
        out_specs=(VMEM, VMEM),
        scratch_shapes=[pltpu.VMEM((t, kv), BF16)],
        cost_estimate=pl.CostEstimate(flops=2 * t * d * kv, bytes_accessed=d * kv, transcendentals=0),
        name="near_products",
    )(at, tokens, upstream, *weights)


def far_products(at, tokens, upstream, acc, sums, weights, scale, group, part=None):
    t, d = tokens.shape
    kv = upstream.shape[1]
    last = part is not None
    rel = pltpu.VMEM((t, kv), BF16)
    if last:
        shapes = (jax.ShapeDtypeStruct((t, kv), BF16), jax.ShapeDtypeStruct((t, d), BF16))
        extra, scratch = (part,), [pltpu.VMEM((t, kv), F32), rel]
    else:
        shapes = (jax.ShapeDtypeStruct((t, kv), F32), jax.ShapeDtypeStruct((t, d // GROUPS), BF16))
        extra, scratch = (), [rel]
    return pl.pallas_call(
        functools.partial(far_kernel, group=group, scale=scale, last=last),
        out_shape=shapes,
        in_specs=[SMEM] + [VMEM] * (6 + len(extra)),
        out_specs=(VMEM, VMEM),
        scratch_shapes=scratch,
        cost_estimate=pl.CostEstimate(flops=t * d * kv, bytes_accessed=d * kv, transcendentals=0),
        name="far_products",
    )(at, tokens, upstream, acc, sums, *weights, *extra)


def step(tokens, upstream, params, momentum, projection):
    rows, _ = params.shape
    n_z, n_xh, n_c = (lax.axis_size(a) for a in FSDP)
    n_isl = lax.axis_size("y") * lax.axis_size("xl")
    fsdp_count = n_z * n_xh * n_c
    width = tokens.shape[1]
    proj = projection.shape[1]
    part = rows // n_isl
    inv_width = 1.0 / math.sqrt(width)
    scale_tok = 1.0 / math.sqrt(tokens.shape[0] * fsdp_count)
    at = jnp.stack([lax.axis_index(a).astype(jnp.int32) for a in ("c", "y", "xh", "xl")])
    swap = functools.partial(lax.ppermute, axis_name="c", perm=[(0, 1), (1, 0)])

    piece = make_piece(at, params, n_z, n_isl)
    got = swap(pick(at, tokens, piece))
    piece = lax.all_to_all(piece, "z", 0, 0, tiled=True)

    q = make_q(upstream, projection)
    got_q = swap(q)
    pair = make_sketch(at, tokens, got, q, got_q, n_z, n_xh)
    along = lax.all_to_all(pair, "z", 0, 0, tiled=True)
    held = split(piece, pair)
    for step in range(3):
        held = join(held, [exchange(h, g, step) for g, h in enumerate(held)])
    far = [exchange(h, g, 3) for g, h in enumerate(held)]
    acc, sums = near_products(at, tokens, upstream, [*held, *(swap(h) for h in held)])
    acc, grads = far_products(at, tokens, upstream, acc, sums, (far[0], swap(far[0])), inv_width, 0)
    values, token_grads = far_products(
        at, tokens, upstream, acc, sums, (far[1], swap(far[1])), inv_width, 1, grads
    )

    along = jnp.sum(along.astype(F32), axis=0).astype(BF16)
    plane = lax.all_to_all(along.reshape(n_xh * n_isl, part, proj), PLANE, 0, 0, tiled=True)
    total = jnp.sum(plane.astype(F32), axis=0).astype(BF16)
    total = jnp.broadcast_to(total[None], (n_isl, part, proj))
    total = lax.all_to_all(total, ISLAND, 0, 0, tiled=True)
    total = total.reshape(rows, proj)

    dims = (((1,), (1,)), ((), ()))
    head, rest = two_parts(projection)
    outer = lax.dot_general(total, head, dims, preferred_element_type=F32)
    outer = outer + lax.dot_general(total, rest, dims, preferred_element_type=F32)
    outer = outer * (scale_tok / (proj * n_isl))
    new_momentum = 0.9 * momentum + outer
    new_params = params - 0.7 * (outer + 0.9 * new_momentum)

    return (values, token_grads, new_params, new_momentum)


def solution(mesh):
    fine = Mesh(mesh.devices.reshape(4, 2, 8, 2, 2), ISLAND + FSDP)
    both = ISLAND + FSDP
    in_specs = (P(both, None), P(both, None), P(FSDP, None), P(FSDP, None), P())
    out_specs = (P(both, None), P(both, None), P(FSDP, None), P(FSDP, None))
    return jax.shard_map(step, mesh=fine, in_specs=in_specs, out_specs=out_specs, check_vma=False)
```

```python
import functools
import math

import jax
import jax.numpy as jnp
from jax import lax
from jax.experimental import pallas as pl
from jax.experimental.pallas import tpu as pltpu
from jax.sharding import Mesh
from jax.sharding import PartitionSpec as P


ISLAND = ("y", "xl")
FSDP = ("z", "xh", "c")
PLANE = ("xh", "y", "xl")
F32, BF16 = jnp.float32, jnp.bfloat16
LANES = 128
VMEM = pl.BlockSpec(memory_space=pltpu.VMEM)
SMEM = pl.BlockSpec(memory_space=pltpu.SMEM)
LEFT = pl.BlockSpec(memory_space=pl.ANY)


def two_parts(x):
    head = x.astype(BF16)
    return head, (x - head.astype(F32)).astype(BF16)


def piece_kernel(at_ref, params_ref, piece_ref):
    width = piece_ref.shape[2]
    block = 2 * at_ref[1] + at_ref[3]
    piece = params_ref[:, pl.ds(pl.multiple_of(block * width, width), width)].astype(BF16)
    for z in range(piece_ref.shape[0]):
        piece_ref[z] = piece


def make_piece(at, params, n_z, pieces):
    rows, kv = params.shape
    return pl.pallas_call(
        piece_kernel,
        out_shape=jax.ShapeDtypeStruct((n_z, rows, kv // pieces), BF16),
        in_specs=[SMEM, VMEM],
        out_specs=VMEM,
        name="make_piece",
    )(at, params)


def pick_kernel(at_ref, tokens_ref, after_ref, out_ref):
    skip = 1 - at_ref[0]
    for k in range(out_ref.shape[1] // LANES):
        at = pl.multiple_of((2 * k + skip) * LANES, LANES)
        out_ref[:, k * LANES : (k + 1) * LANES] = tokens_ref[:, pl.ds(at, LANES)]


def pick(at, tokens, after):
    t, d = tokens.shape
    return pl.pallas_call(
        pick_kernel,
        out_shape=jax.ShapeDtypeStruct((t, d // 2), BF16),
        in_specs=[SMEM, VMEM, LEFT],
        out_specs=VMEM,
        name="pick",
    )(at, tokens, after)


def q_kernel(up_ref, proj_ref, q_ref):
    head, rest = two_parts(proj_ref[...])
    q = jnp.dot(up_ref[...], head, preferred_element_type=F32)
    q += jnp.dot(up_ref[...], rest, preferred_element_type=F32)
    q_ref[...] = q.astype(BF16)


def make_q(upstream, projection):
    return pl.pallas_call(
        q_kernel,
        out_shape=jax.ShapeDtypeStruct((upstream.shape[0], projection.shape[1]), BF16),
        in_specs=[VMEM, VMEM],
        out_specs=VMEM,
        cost_estimate=pl.CostEstimate(
            flops=8 * upstream.size * projection.shape[1],
            bytes_accessed=4 * projection.size + 4 * upstream.size,
            transcendentals=0,
        ),
        name="make_q",
    )(upstream, projection)


def sketch_kernel(at_ref, tok_ref, got_ref, q_ref, got_q_ref, out_ref):
    n_z, n_xh = out_ref.shape[:2]
    dims = (((0,), (0,)), ((), ()))
    for k in range(n_z * n_xh):
        mine = tok_ref[:, pl.ds(pl.multiple_of((2 * k + at_ref[0]) * LANES, LANES), LANES)]
        theirs = got_ref[:, k * LANES : (k + 1) * LANES]
        s = lax.dot_general(mine, q_ref[...], dims, preferred_element_type=F32)
        s += lax.dot_general(theirs, got_q_ref[...], dims, preferred_element_type=F32)
        out_ref[k // n_xh, k % n_xh] = s.astype(BF16)


def make_sketch(at, tokens, got, q, got_q, n_z, n_xh):
    proj = q.shape[1]
    return pl.pallas_call(
        sketch_kernel,
        out_shape=jax.ShapeDtypeStruct((n_z, n_xh, LANES, proj), BF16),
        in_specs=[SMEM] + [VMEM] * 4,
        out_specs=VMEM,
        cost_estimate=pl.CostEstimate(
            flops=8 * tokens.size * proj, bytes_accessed=16 * tokens.size, transcendentals=0
        ),
        name="make_sketch",
    )(at, tokens, got, q, got_q)


ORDERS = (("XALB", "LBXA"), ("ALBX", "BXAL"))
GROUPS = len(ORDERS[0])
FLIP = {"X": (1, 0, 1), "L": (0, 0, 1), "A": (0, 1, 0), "B": (0, 3, 0)}


def exchange(x, group, step):
    def index(y, xl, xh, c):
        return ((y * 2 + xl) * 2 + xh) * 2 + c

    pairs = []
    for y in range(4):
        for xl in range(2):
            for xh in range(2):
                for c in range(2):
                    a, b, l = FLIP[ORDERS[c][group][step]]
                    pairs.append((index(y, xl, xh, c), index(y ^ b, xl ^ l, xh ^ a, c)))
    return lax.ppermute(x, ("y", "xl", "xh", "c"), pairs)


def places(core, group):
    order = ORDERS[core][group]
    held = [(0, 0, 0)]
    for kind in order[:3]:
        f = FLIP[kind]
        held = held + [(a ^ f[0], b ^ f[1], l ^ f[2]) for a, b, l in held]
    f = FLIP[order[3]]
    far = [(a ^ f[0], b ^ f[1], l ^ f[2]) for a, b, l in held]
    return {
        (half, a): sorted(((b, l), i) for i, (a_, b, l) in enumerate(part) if a_ == a)
        for half, part in enumerate((held, far))
        for a in range(2)
    }


def split_kernel(piece_ref, after_ref, *out_refs):
    each = out_refs[0].shape[0]
    for g, out_ref in enumerate(out_refs):
        out_ref[...] = piece_ref[g * each : (g + 1) * each]


def split(piece, after):
    n = GROUPS
    shape = (piece.shape[0] // n,) + piece.shape[1:]
    return pl.pallas_call(
        split_kernel,
        out_shape=(jax.ShapeDtypeStruct(shape, BF16),) * n,
        in_specs=[VMEM, LEFT],
        out_specs=(VMEM,) * n,
        name="split",
    )(piece, after)


def lanes(ref, blocks):
    return jnp.concatenate([ref[:, at] for at in blocks], axis=1)


def half_products(half, groups, core, at_ref, tok_ref, w_refs, acc_ref, up_rel, take):
    xh = at_ref[2]
    each = w_refs[0].shape[0] // 8
    for n, g in enumerate(groups):
        for o in range(2):
            table = places(core ^ o, g)
            w_ref = w_refs[len(groups) * o + n]
            for a in range(2):
                zs = range(g * each, (g + 1) * each)
                blocks = [
                    pl.ds(pl.multiple_of((2 * (2 * z + (xh ^ a)) + (core ^ o)) * LANES, LANES), LANES) for z in zs
                ]
                found = table[half, a]
                total = None
                if found:
                    w = jnp.concatenate(
                        [
                            jnp.concatenate([w_ref[i * each + k] for _, i in found], axis=1)
                            for k in range(each)
                        ],
                        axis=0,
                    )
                    here = [slice((2 * b + l) * LANES, (2 * b + l + 1) * LANES) for (b, l), _ in found]
                    part = jnp.dot(lanes(tok_ref, blocks), w, preferred_element_type=F32)
                    for i, at in enumerate(here):
                        acc_ref[:, at] += part[:, i * LANES : (i + 1) * LANES]
                    total = lax.dot_general(
                        lanes(up_rel, here), w, (((1,), (1,)), ((), ())), preferred_element_type=F32
                    )
                take(g, a, o, blocks, total)


def columns(at_ref):
    y, xl = at_ref[1], at_ref[3]
    return [
        pl.ds(pl.multiple_of((2 * (y ^ (r // 2)) + (xl ^ (r % 2))) * LANES, LANES), LANES) for r in range(8)
    ]


def arrange(at_ref, up_ref, up_rel):
    for r, at in enumerate(columns(at_ref)):
        up_rel[:, r * LANES : (r + 1) * LANES] = up_ref[:, at]


def near_kernel(at_ref, tok_ref, up_ref, *refs):
    w_refs, (acc_ref, *sum_refs, up_rel) = refs[: 2 * GROUPS], refs[2 * GROUPS :]
    acc_ref[...] = jnp.zeros(acc_ref.shape, F32)
    arrange(at_ref, up_ref, up_rel)

    def take(g, a, o, blocks, total):
        if total is not None:
            sum_refs[g][2 * a + o] = total

    for core in range(2):

        @pl.when(at_ref[0] == core)
        def _():
            half_products(0, range(GROUPS), core, at_ref, tok_ref, w_refs, acc_ref, up_rel, take)


def far_kernel(at_ref, tok_ref, up_ref, before_ref, sum_ref, *refs, group, scale, last):
    w_refs = refs[:2]
    if last:
        part_ref, values_ref, grads_ref, acc_ref, up_rel = refs[2:]
        done = part_ref.shape[1]
        grads_ref[:, :done] = part_ref[...]
    else:
        acc_ref, grads_ref, up_rel = refs[2:]
    acc_ref[...] = before_ref[...]
    arrange(at_ref, up_ref, up_rel)

    for core in range(2):

        def take(g, a, o, blocks, total, core=core):
            if places(core ^ o, g)[0, a]:
                before = sum_ref[2 * a + o]
                total = before if total is None else total + before
            grad = (total * scale).astype(BF16)
            for k, at in enumerate(blocks):
                grads_ref[:, at] = grad[:, k * LANES : (k + 1) * LANES]

        @pl.when(at_ref[0] == core)
        def _():
            half_products(1, (group,), core, at_ref, tok_ref, w_refs, acc_ref, up_rel, take)

    if last:
        for r, at in enumerate(columns(at_ref)):
            values_ref[:, at] = (acc_ref[:, r * LANES : (r + 1) * LANES] * scale).astype(BF16)


def near_products(at, tokens, upstream, weights):
    t, d = tokens.shape
    kv = upstream.shape[1]
    return pl.pallas_call(
        near_kernel,
        out_shape=(
            jax.ShapeDtypeStruct((t, kv), F32),
            *[jax.ShapeDtypeStruct((4, t, d // (4 * GROUPS)), F32)] * GROUPS,
        ),
        in_specs=[SMEM] + [VMEM] * (2 + len(weights)),
        out_specs=(VMEM,) * (1 + GROUPS),
        scratch_shapes=[pltpu.VMEM((t, kv), BF16)],
        cost_estimate=pl.CostEstimate(flops=2 * t * d * kv, bytes_accessed=d * kv, transcendentals=0),
        name="near_products",
    )(at, tokens, upstream, *weights)


def far_products(at, tokens, upstream, acc, sums, weights, scale, group, part=None):
    t, d = tokens.shape
    kv = upstream.shape[1]
    last = part is not None
    rel = pltpu.VMEM((t, kv), BF16)
    if last:
        shapes = (jax.ShapeDtypeStruct((t, kv), BF16), jax.ShapeDtypeStruct((t, d), BF16))
        extra, scratch = (part,), [pltpu.VMEM((t, kv), F32), rel]
    else:
        shapes = (jax.ShapeDtypeStruct((t, kv), F32), jax.ShapeDtypeStruct((t, d // GROUPS), BF16))
        extra, scratch = (), [rel]
    return pl.pallas_call(
        functools.partial(far_kernel, group=group, scale=scale, last=last),
        out_shape=shapes,
        in_specs=[SMEM] + [VMEM] * (6 + len(extra)),
        out_specs=(VMEM, VMEM),
        scratch_shapes=scratch,
        cost_estimate=pl.CostEstimate(flops=t * d * kv, bytes_accessed=d * kv, transcendentals=0),
        name="far_products",
    )(at, tokens, upstream, acc, sums, *weights, *extra)


def step(tokens, upstream, params, momentum, projection):
    rows, _ = params.shape
    n_z, n_xh, n_c = (lax.axis_size(a) for a in FSDP)
    n_isl = lax.axis_size("y") * lax.axis_size("xl")
    fsdp_count = n_z * n_xh * n_c
    width = tokens.shape[1]
    proj = projection.shape[1]
    part = rows // n_isl
    inv_width = 1.0 / math.sqrt(width)
    scale_tok = 1.0 / math.sqrt(tokens.shape[0] * fsdp_count)
    at = jnp.stack([lax.axis_index(a).astype(jnp.int32) for a in ("c", "y", "xh", "xl")])
    swap = functools.partial(lax.ppermute, axis_name="c", perm=[(0, 1), (1, 0)])

    piece = make_piece(at, params, n_z, n_isl)
    other = pick(at, tokens, piece)
    got = swap(other)
    piece = lax.all_to_all(piece, "z", 0, 0, tiled=True)

    q = make_q(upstream, projection)
    got_q = swap(q)
    pair = make_sketch(at, tokens, got, q, got_q, n_z, n_xh)
    along = lax.all_to_all(pair, "z", 0, 0, tiled=True)
    held = split(piece, pair)
    for step in range(3):
        held = [jnp.concatenate([h, exchange(h, g, step)], axis=0) for g, h in enumerate(held)]
    far = [exchange(h, g, 3) for g, h in enumerate(held)]
    acc, *sums = near_products(at, tokens, upstream, [*held, *(swap(h) for h in held)])
    acc, grads = far_products(
        at, tokens, upstream, acc, sums[0], (far[0], swap(far[0])), inv_width, 0
    )
    values, token_grads = far_products(
        at, tokens, upstream, acc, sums[1], (far[1], swap(far[1])), inv_width, 1, grads
    )

    along = jnp.sum(along.astype(F32), axis=0).astype(BF16)
    plane = lax.all_to_all(along.reshape(n_xh * n_isl, part, proj), PLANE, 0, 0, tiled=True)
    total = jnp.sum(plane.astype(F32), axis=0).astype(BF16)
    total = jnp.broadcast_to(total[None], (n_isl, part, proj))
    total = lax.all_to_all(total, ISLAND, 0, 0, tiled=True)
    total = total.reshape(rows, proj)

    dims = (((1,), (1,)), ((), ()))
    head, rest = two_parts(projection)
    outer = lax.dot_general(total, head, dims, preferred_element_type=F32)
    outer = outer + lax.dot_general(total, rest, dims, preferred_element_type=F32)
    outer = outer * (scale_tok / (proj * n_isl))
    new_momentum = 0.9 * momentum + outer
    new_params = params - 0.7 * (outer + 0.9 * new_momentum)

    return (values, token_grads, new_params, new_momentum)


def solution(mesh):
    fine = Mesh(mesh.devices.reshape(4, 2, 8, 2, 2), ISLAND + FSDP)
    both = ISLAND + FSDP
    in_specs = (P(both, None), P(both, None), P(FSDP, None), P(FSDP, None), P())
    out_specs = (P(both, None), P(both, None), P(FSDP, None), P(FSDP, None))
    return jax.shard_map(step, mesh=fine, in_specs=in_specs, out_specs=out_specs, check_vma=False)
```

```python
import functools
import math

import jax
import jax.numpy as jnp
from jax import lax
from jax.experimental import pallas as pl
from jax.experimental.pallas import tpu as pltpu
from jax.sharding import Mesh
from jax.sharding import PartitionSpec as P


ISLAND = ("y", "xl")
FSDP = ("z", "xh", "c")
PLANE = ("xh", "y", "xl")
F32, BF16 = jnp.float32, jnp.bfloat16
LANES = 128
VMEM = pl.BlockSpec(memory_space=pltpu.VMEM)
SMEM = pl.BlockSpec(memory_space=pltpu.SMEM)
LEFT = pl.BlockSpec(memory_space=pl.ANY)


def two_parts(x):
    head = x.astype(BF16)
    return head, (x - head.astype(F32)).astype(BF16)


def piece_kernel(at_ref, params_ref, piece_ref):
    width = piece_ref.shape[2]
    block = 2 * at_ref[1] + at_ref[3]
    piece = params_ref[:, pl.ds(pl.multiple_of(block * width, width), width)].astype(BF16)
    for z in range(piece_ref.shape[0]):
        piece_ref[z] = piece


def make_piece(at, params, n_z, pieces):
    rows, kv = params.shape
    return pl.pallas_call(
        piece_kernel,
        out_shape=jax.ShapeDtypeStruct((n_z, rows, kv // pieces), BF16),
        in_specs=[SMEM, VMEM],
        out_specs=VMEM,
        name="make_piece",
    )(at, params)


def pick_kernel(at_ref, tokens_ref, after_ref, out_ref):
    skip = 1 - at_ref[0]
    for k in range(out_ref.shape[1] // LANES):
        at = pl.multiple_of((2 * k + skip) * LANES, LANES)
        out_ref[:, k * LANES : (k + 1) * LANES] = tokens_ref[:, pl.ds(at, LANES)]


def pick(at, tokens, after):
    t, d = tokens.shape
    return pl.pallas_call(
        pick_kernel,
        out_shape=jax.ShapeDtypeStruct((t, d // 2), BF16),
        in_specs=[SMEM, VMEM, LEFT],
        out_specs=VMEM,
        name="pick",
    )(at, tokens, after)


def q_kernel(up_ref, proj_ref, q_ref):
    head, rest = two_parts(proj_ref[...])
    q = jnp.dot(up_ref[...], head, preferred_element_type=F32)
    q += jnp.dot(up_ref[...], rest, preferred_element_type=F32)
    q_ref[...] = q.astype(BF16)


def make_q(upstream, projection):
    return pl.pallas_call(
        q_kernel,
        out_shape=jax.ShapeDtypeStruct((upstream.shape[0], projection.shape[1]), BF16),
        in_specs=[VMEM, VMEM],
        out_specs=VMEM,
        cost_estimate=pl.CostEstimate(
            flops=8 * upstream.size * projection.shape[1],
            bytes_accessed=4 * projection.size + 4 * upstream.size,
            transcendentals=0,
        ),
        name="make_q",
    )(upstream, projection)


def sketch_kernel(at_ref, tok_ref, got_ref, q_ref, got_q_ref, *out_refs):
    n_z = len(out_refs)
    n_xh = out_refs[0].shape[0]
    dims = (((0,), (0,)), ((), ()))
    for r, out_ref in enumerate(out_refs):
        z = lax.rem(at_ref[4] + r, n_z)
        for h in range(n_xh):
            k = z * n_xh + h
            mine = tok_ref[:, pl.ds(pl.multiple_of((2 * k + at_ref[0]) * LANES, LANES), LANES)]
            theirs = got_ref[:, pl.ds(pl.multiple_of(k * LANES, LANES), LANES)]
            s = lax.dot_general(mine, q_ref[...], dims, preferred_element_type=F32)
            s += lax.dot_general(theirs, got_q_ref[...], dims, preferred_element_type=F32)
            out_ref[h] = s.astype(BF16)


def make_sketch(at, tokens, got, q, got_q, n_z, n_xh):
    proj = q.shape[1]
    return pl.pallas_call(
        sketch_kernel,
        out_shape=(jax.ShapeDtypeStruct((n_xh, LANES, proj), BF16),) * n_z,
        in_specs=[SMEM] + [VMEM] * 4,
        out_specs=(VMEM,) * n_z,
        cost_estimate=pl.CostEstimate(
            flops=8 * tokens.size * proj, bytes_accessed=16 * tokens.size, transcendentals=0
        ),
        name="make_sketch",
    )(at, tokens, got, q, got_q)


ORDERS = (("XALB", "LBXA"), ("ALBX", "BXAL"))
GROUPS = len(ORDERS[0])
FLIP = {"X": (1, 0, 1), "L": (0, 0, 1), "A": (0, 1, 0), "B": (0, 3, 0)}


def exchange(x, group, step):
    def index(y, xl, xh, c):
        return ((y * 2 + xl) * 2 + xh) * 2 + c

    pairs = []
    for y in range(4):
        for xl in range(2):
            for xh in range(2):
                for c in range(2):
                    a, b, l = FLIP[ORDERS[c][group][step]]
                    pairs.append((index(y, xl, xh, c), index(y ^ b, xl ^ l, xh ^ a, c)))
    return lax.ppermute(x, ("y", "xl", "xh", "c"), pairs)


def places(core, group):
    order = ORDERS[core][group]
    held = [(0, 0, 0)]
    for kind in order[:3]:
        f = FLIP[kind]
        held = held + [(a ^ f[0], b ^ f[1], l ^ f[2]) for a, b, l in held]
    f = FLIP[order[3]]
    far = [(a ^ f[0], b ^ f[1], l ^ f[2]) for a, b, l in held]
    return {
        (half, a): sorted(((b, l), i) for i, (a_, b, l) in enumerate(part) if a_ == a)
        for half, part in enumerate((held, far))
        for a in range(2)
    }


def split_kernel(piece_ref, after_ref, *out_refs):
    each = out_refs[0].shape[0]
    for g, out_ref in enumerate(out_refs):
        out_ref[...] = piece_ref[g * each : (g + 1) * each]


def split(piece, after):
    n = GROUPS
    shape = (piece.shape[0] // n,) + piece.shape[1:]
    return pl.pallas_call(
        split_kernel,
        out_shape=(jax.ShapeDtypeStruct(shape, BF16),) * n,
        in_specs=[VMEM, LEFT],
        out_specs=(VMEM,) * n,
        name="split",
    )(piece, after)


def lanes(ref, blocks):
    return jnp.concatenate([ref[:, at] for at in blocks], axis=1)


def half_products(half, groups, core, at_ref, tok_ref, w_refs, acc_ref, up_rel, take):
    xh = at_ref[2]
    each = w_refs[0].shape[0] // 8
    for n, g in enumerate(groups):
        for o in range(2):
            table = places(core ^ o, g)
            w_ref = w_refs[len(groups) * o + n]
            for a in range(2):
                zs = range(g * each, (g + 1) * each)
                blocks = [
                    pl.ds(pl.multiple_of((2 * (2 * z + (xh ^ a)) + (core ^ o)) * LANES, LANES), LANES) for z in zs
                ]
                found = table[half, a]
                total = None
                if found:
                    w = jnp.concatenate(
                        [
                            jnp.concatenate([w_ref[i * each + k] for _, i in found], axis=1)
                            for k in range(each)
                        ],
                        axis=0,
                    )
                    here = [slice((2 * b + l) * LANES, (2 * b + l + 1) * LANES) for (b, l), _ in found]
                    part = jnp.dot(lanes(tok_ref, blocks), w, preferred_element_type=F32)
                    for i, at in enumerate(here):
                        acc_ref[:, at] += part[:, i * LANES : (i + 1) * LANES]
                    total = lax.dot_general(
                        lanes(up_rel, here), w, (((1,), (1,)), ((), ())), preferred_element_type=F32
                    )
                take(g, a, o, blocks, total)


def columns(at_ref):
    y, xl = at_ref[1], at_ref[3]
    return [
        pl.ds(pl.multiple_of((2 * (y ^ (r // 2)) + (xl ^ (r % 2))) * LANES, LANES), LANES) for r in range(8)
    ]


def arrange(at_ref, up_ref, up_rel):
    for r, at in enumerate(columns(at_ref)):
        up_rel[:, r * LANES : (r + 1) * LANES] = up_ref[:, at]


def near_kernel(at_ref, tok_ref, up_ref, *refs):
    w_refs, (acc_ref, *sum_refs, up_rel) = refs[: 2 * GROUPS], refs[2 * GROUPS :]
    acc_ref[...] = jnp.zeros(acc_ref.shape, F32)
    arrange(at_ref, up_ref, up_rel)

    def take(g, a, o, blocks, total):
        if total is not None:
            sum_refs[g][2 * a + o] = total

    for core in range(2):

        @pl.when(at_ref[0] == core)
        def _():
            half_products(0, range(GROUPS), core, at_ref, tok_ref, w_refs, acc_ref, up_rel, take)


def far_kernel(at_ref, tok_ref, up_ref, before_ref, *refs, scale):
    sum_refs, w_refs = refs[:GROUPS], refs[GROUPS : 3 * GROUPS]
    values_ref, grads_ref, acc_ref, up_rel = refs[3 * GROUPS :]
    acc_ref[...] = before_ref[...]
    arrange(at_ref, up_ref, up_rel)

    for core in range(2):

        def take(g, a, o, blocks, total, core=core):
            if places(core ^ o, g)[0, a]:
                before = sum_refs[g][2 * a + o]
                total = before if total is None else total + before
            grad = (total * scale).astype(BF16)
            for k, at in enumerate(blocks):
                grads_ref[:, at] = grad[:, k * LANES : (k + 1) * LANES]

        @pl.when(at_ref[0] == core)
        def _():
            half_products(1, range(GROUPS), core, at_ref, tok_ref, w_refs, acc_ref, up_rel, take)

    for r, at in enumerate(columns(at_ref)):
        values_ref[:, at] = (acc_ref[:, r * LANES : (r + 1) * LANES] * scale).astype(BF16)


def near_products(at, tokens, upstream, weights):
    t, d = tokens.shape
    kv = upstream.shape[1]
    return pl.pallas_call(
        near_kernel,
        out_shape=(
            jax.ShapeDtypeStruct((t, kv), F32),
            *[jax.ShapeDtypeStruct((4, t, d // (4 * GROUPS)), F32)] * GROUPS,
        ),
        in_specs=[SMEM] + [VMEM] * (2 + len(weights)),
        out_specs=(VMEM,) * (1 + GROUPS),
        scratch_shapes=[pltpu.VMEM((t, kv), BF16)],
        cost_estimate=pl.CostEstimate(flops=2 * t * d * kv, bytes_accessed=d * kv, transcendentals=0),
        name="near_products",
    )(at, tokens, upstream, *weights)


def far_products(at, tokens, upstream, acc, sums, weights, scale):
    t, d = tokens.shape
    kv = upstream.shape[1]
    return pl.pallas_call(
        functools.partial(far_kernel, scale=scale),
        out_shape=(jax.ShapeDtypeStruct((t, kv), BF16), jax.ShapeDtypeStruct((t, d), BF16)),
        in_specs=[SMEM] + [VMEM] * (3 + len(sums) + len(weights)),
        out_specs=(VMEM, VMEM),
        scratch_shapes=[pltpu.VMEM((t, kv), F32), pltpu.VMEM((t, kv), BF16)],
        cost_estimate=pl.CostEstimate(flops=2 * t * d * kv, bytes_accessed=d * kv, transcendentals=0),
        name="far_products",
    )(at, tokens, upstream, acc, *sums, *weights)


def step(tokens, upstream, params, momentum, projection):
    rows, _ = params.shape
    n_z, n_xh, n_c = (lax.axis_size(a) for a in FSDP)
    n_isl = lax.axis_size("y") * lax.axis_size("xl")
    fsdp_count = n_z * n_xh * n_c
    width = tokens.shape[1]
    proj = projection.shape[1]
    part = rows // n_isl
    inv_width = 1.0 / math.sqrt(width)
    scale_tok = 1.0 / math.sqrt(tokens.shape[0] * fsdp_count)
    at = jnp.stack([lax.axis_index(a).astype(jnp.int32) for a in ("c", "y", "xh", "xl", "z")])
    swap = functools.partial(lax.ppermute, axis_name="c", perm=[(0, 1), (1, 0)])

    piece = make_piece(at, params, n_z, n_isl)
    other = pick(at, tokens, piece)
    got = swap(other)
    piece = lax.all_to_all(piece, "z", 0, 0, tiled=True)

    q = make_q(upstream, projection)
    got_q = swap(q)
    pair = make_sketch(at, tokens, got, q, got_q, n_z, n_xh)

    def shift(x, k):
        return lax.ppermute(x, "z", [(i, (i + k) % n_z) for i in range(n_z)])

    half_way = n_z // 2
    near_by = half_way + 1
    relayed = shift(pair[half_way], n_z - 1)
    along = pair[0].astype(F32)
    for k in range(half_way - 1, 0, -1):
        along += shift(pair[k], k).astype(F32)
        if k < half_way - 1:
            along += shift(pair[n_z - k], n_z - k).astype(F32)
    joined = (pair[near_by].astype(F32) + relayed.astype(F32)).astype(BF16)
    along += shift(joined, near_by).astype(F32)
    held = split(piece, pair[0])
    for step in range(3):
        more = [exchange(h, g, step) for g, h in enumerate(held)]
        held = [jnp.concatenate(both, axis=0) for both in zip(held, more)]
    far = [exchange(h, g, 3) for g, h in enumerate(held)]
    acc, *sums = near_products(at, tokens, upstream, [*held, *(swap(h) for h in held)])
    values, token_grads = far_products(
        at, tokens, upstream, acc, sums, [*far, *(swap(f) for f in far)], inv_width
    )

    along = along.astype(BF16)
    plane = lax.all_to_all(along.reshape(n_xh * n_isl, part, proj), PLANE, 0, 0, tiled=True)
    total = jnp.sum(plane.astype(F32), axis=0).astype(BF16)
    total = jnp.broadcast_to(total[None], (n_isl, part, proj))
    total = lax.all_to_all(total, ISLAND, 0, 0, tiled=True)
    total = total.reshape(rows, proj)

    dims = (((1,), (1,)), ((), ()))
    head, rest = two_parts(projection)
    outer = lax.dot_general(total, head, dims, preferred_element_type=F32)
    outer = outer + lax.dot_general(total, rest, dims, preferred_element_type=F32)
    outer = outer * (scale_tok / (proj * n_isl))
    new_momentum = 0.9 * momentum + outer
    new_params = params - 0.7 * (outer + 0.9 * new_momentum)

    return (values, token_grads, new_params, new_momentum)


def solution(mesh):
    fine = Mesh(mesh.devices.reshape(4, 2, 8, 2, 2), ISLAND + FSDP)
    both = ISLAND + FSDP
    in_specs = (P(both, None), P(both, None), P(FSDP, None), P(FSDP, None), P())
    out_specs = (P(both, None), P(both, None), P(FSDP, None), P(FSDP, None))
    return jax.shard_map(step, mesh=fine, in_specs=in_specs, out_specs=out_specs, check_vma=False)
```

```python
import functools
import math

import jax
import jax.numpy as jnp
from jax import lax
from jax.experimental import pallas as pl
from jax.experimental.pallas import tpu as pltpu
from jax.sharding import Mesh
from jax.sharding import PartitionSpec as P


ISLAND = ("y", "xl")
FSDP = ("z", "xh", "c")
PLANE = ("xh", "y", "xl")
F32, BF16 = jnp.float32, jnp.bfloat16
LANES = 128
VMEM = pl.BlockSpec(memory_space=pltpu.VMEM)
SMEM = pl.BlockSpec(memory_space=pltpu.SMEM)
LEFT = pl.BlockSpec(memory_space=pl.ANY)


def two_parts(x):
    head = x.astype(BF16)
    return head, (x - head.astype(F32)).astype(BF16)


def piece_kernel(at_ref, params_ref, piece_ref):
    width = piece_ref.shape[2]
    block = 2 * at_ref[1] + at_ref[3]
    piece = params_ref[:, pl.ds(pl.multiple_of(block * width, width), width)].astype(BF16)
    for z in range(piece_ref.shape[0]):
        piece_ref[z] = piece


def make_piece(at, params, n_z, pieces):
    rows, kv = params.shape
    return pl.pallas_call(
        piece_kernel,
        out_shape=jax.ShapeDtypeStruct((n_z, rows, kv // pieces), BF16),
        in_specs=[SMEM, VMEM],
        out_specs=VMEM,
        name="make_piece",
    )(at, params)


def pick_kernel(at_ref, tokens_ref, after_ref, out_ref):
    skip = 1 - at_ref[0]
    for k in range(out_ref.shape[1] // LANES):
        at = pl.multiple_of((2 * k + skip) * LANES, LANES)
        out_ref[:, k * LANES : (k + 1) * LANES] = tokens_ref[:, pl.ds(at, LANES)]


def pick(at, tokens, after):
    t, d = tokens.shape
    return pl.pallas_call(
        pick_kernel,
        out_shape=jax.ShapeDtypeStruct((t, d // 2), BF16),
        in_specs=[SMEM, VMEM, LEFT],
        out_specs=VMEM,
        name="pick",
    )(at, tokens, after)


def q_kernel(up_ref, proj_ref, q_ref):
    head, rest = two_parts(proj_ref[...])
    q = jnp.dot(up_ref[...], head, preferred_element_type=F32)
    q += jnp.dot(up_ref[...], rest, preferred_element_type=F32)
    q_ref[...] = q.astype(BF16)


def make_q(upstream, projection):
    return pl.pallas_call(
        q_kernel,
        out_shape=jax.ShapeDtypeStruct((upstream.shape[0], projection.shape[1]), BF16),
        in_specs=[VMEM, VMEM],
        out_specs=VMEM,
        cost_estimate=pl.CostEstimate(
            flops=8 * upstream.size * projection.shape[1],
            bytes_accessed=4 * projection.size + 4 * upstream.size,
            transcendentals=0,
        ),
        name="make_q",
    )(upstream, projection)


def sketch_kernel(at_ref, tok_ref, got_ref, q_ref, got_q_ref, *out_refs):
    n_z = len(out_refs)
    n_xh = out_refs[0].shape[0]
    dims = (((0,), (0,)), ((), ()))
    for r, out_ref in enumerate(out_refs):
        z = lax.rem(at_ref[4] + r, n_z)
        for h in range(n_xh):
            k = z * n_xh + h
            mine = tok_ref[:, pl.ds(pl.multiple_of((2 * k + at_ref[0]) * LANES, LANES), LANES)]
            theirs = got_ref[:, pl.ds(pl.multiple_of(k * LANES, LANES), LANES)]
            s = lax.dot_general(mine, q_ref[...], dims, preferred_element_type=F32)
            s += lax.dot_general(theirs, got_q_ref[...], dims, preferred_element_type=F32)
            out_ref[h] = s.astype(BF16)


def make_sketch(at, tokens, got, q, got_q, n_z, n_xh):
    proj = q.shape[1]
    return pl.pallas_call(
        sketch_kernel,
        out_shape=(jax.ShapeDtypeStruct((n_xh, LANES, proj), BF16),) * n_z,
        in_specs=[SMEM] + [VMEM] * 4,
        out_specs=(VMEM,) * n_z,
        cost_estimate=pl.CostEstimate(
            flops=8 * tokens.size * proj, bytes_accessed=16 * tokens.size, transcendentals=0
        ),
        name="make_sketch",
    )(at, tokens, got, q, got_q)


ORDERS = (("XALB", "LBXA"), ("ALBX", "BXAL"))
GROUPS = len(ORDERS[0])
FLIP = {"X": (1, 0, 1), "L": (0, 0, 1), "A": (0, 1, 0), "B": (0, 3, 0)}


def exchange(x, group, step):
    def index(y, xl, xh, c):
        return ((y * 2 + xl) * 2 + xh) * 2 + c

    pairs = []
    for y in range(4):
        for xl in range(2):
            for xh in range(2):
                for c in range(2):
                    a, b, l = FLIP[ORDERS[c][group][step]]
                    pairs.append((index(y, xl, xh, c), index(y ^ b, xl ^ l, xh ^ a, c)))
    return lax.ppermute(x, ("y", "xl", "xh", "c"), pairs)


def places(core, group):
    order = ORDERS[core][group]
    held = [(0, 0, 0)]
    for kind in order[:3]:
        f = FLIP[kind]
        held = held + [(a ^ f[0], b ^ f[1], l ^ f[2]) for a, b, l in held]
    f = FLIP[order[3]]
    far = [(a ^ f[0], b ^ f[1], l ^ f[2]) for a, b, l in held]
    return {
        (half, a): sorted(((b, l), i) for i, (a_, b, l) in enumerate(part) if a_ == a)
        for half, part in enumerate((held, far))
        for a in range(2)
    }


def lanes(ref, blocks):
    return jnp.concatenate([ref[:, at] for at in blocks], axis=1)


def half_products(half, groups, core, at_ref, tok_ref, w_refs, acc_ref, up_rel, take):
    xh = at_ref[2]
    each = w_refs[0].shape[0] // 8
    for n, g in enumerate(groups):
        for o in range(2):
            table = places(core ^ o, g)
            w_ref = w_refs[len(groups) * o + n]
            for a in range(2):
                zs = range(g * each, (g + 1) * each)
                blocks = [
                    pl.ds(pl.multiple_of((2 * (2 * z + (xh ^ a)) + (core ^ o)) * LANES, LANES), LANES) for z in zs
                ]
                found = table[half, a]
                total = None
                if found:
                    w = jnp.concatenate(
                        [
                            jnp.concatenate([w_ref[i * each + k] for _, i in found], axis=1)
                            for k in range(each)
                        ],
                        axis=0,
                    )
                    here = [slice((2 * b + l) * LANES, (2 * b + l + 1) * LANES) for (b, l), _ in found]
                    part = jnp.dot(lanes(tok_ref, blocks), w, preferred_element_type=F32)
                    for i, at in enumerate(here):
                        acc_ref[:, at] += part[:, i * LANES : (i + 1) * LANES]
                    total = lax.dot_general(
                        lanes(up_rel, here), w, (((1,), (1,)), ((), ())), preferred_element_type=F32
                    )
                take(g, a, o, blocks, total)


def columns(at_ref):
    y, xl = at_ref[1], at_ref[3]
    return [
        pl.ds(pl.multiple_of((2 * (y ^ (r // 2)) + (xl ^ (r % 2))) * LANES, LANES), LANES) for r in range(8)
    ]


def arrange(at_ref, up_ref, up_rel):
    for r, at in enumerate(columns(at_ref)):
        up_rel[:, r * LANES : (r + 1) * LANES] = up_ref[:, at]


def near_kernel(at_ref, tok_ref, up_ref, *refs):
    w_refs, (acc_ref, *sum_refs, up_rel) = refs[: 2 * GROUPS], refs[2 * GROUPS :]
    acc_ref[...] = jnp.zeros(acc_ref.shape, F32)
    arrange(at_ref, up_ref, up_rel)

    def take(g, a, o, blocks, total):
        if total is not None:
            sum_refs[g][2 * a + o] = total

    for core in range(2):

        @pl.when(at_ref[0] == core)
        def _():
            half_products(0, range(GROUPS), core, at_ref, tok_ref, w_refs, acc_ref, up_rel, take)


def far_kernel(at_ref, tok_ref, up_ref, before_ref, *refs, scale):
    sum_refs, w_refs = refs[:GROUPS], refs[GROUPS : 3 * GROUPS]
    values_ref, grads_ref, acc_ref, up_rel = refs[3 * GROUPS :]
    acc_ref[...] = before_ref[...]
    arrange(at_ref, up_ref, up_rel)

    for core in range(2):

        def take(g, a, o, blocks, total, core=core):
            if places(core ^ o, g)[0, a]:
                before = sum_refs[g][2 * a + o]
                total = before if total is None else total + before
            grad = (total * scale).astype(BF16)
            for k, at in enumerate(blocks):
                grads_ref[:, at] = grad[:, k * LANES : (k + 1) * LANES]

        @pl.when(at_ref[0] == core)
        def _():
            half_products(1, range(GROUPS), core, at_ref, tok_ref, w_refs, acc_ref, up_rel, take)

    for r, at in enumerate(columns(at_ref)):
        values_ref[:, at] = (acc_ref[:, r * LANES : (r + 1) * LANES] * scale).astype(BF16)


def near_products(at, tokens, upstream, weights):
    t, d = tokens.shape
    kv = upstream.shape[1]
    return pl.pallas_call(
        near_kernel,
        out_shape=(
            jax.ShapeDtypeStruct((t, kv), F32),
            *[jax.ShapeDtypeStruct((4, t, d // (4 * GROUPS)), F32)] * GROUPS,
        ),
        in_specs=[SMEM] + [VMEM] * (2 + len(weights)),
        out_specs=(VMEM,) * (1 + GROUPS),
        scratch_shapes=[pltpu.VMEM((t, kv), BF16)],
        cost_estimate=pl.CostEstimate(flops=2 * t * d * kv, bytes_accessed=d * kv, transcendentals=0),
        name="near_products",
    )(at, tokens, upstream, *weights)


def far_products(at, tokens, upstream, acc, sums, weights, scale):
    t, d = tokens.shape
    kv = upstream.shape[1]
    return pl.pallas_call(
        functools.partial(far_kernel, scale=scale),
        out_shape=(jax.ShapeDtypeStruct((t, kv), BF16), jax.ShapeDtypeStruct((t, d), BF16)),
        in_specs=[SMEM] + [VMEM] * (3 + len(sums) + len(weights)),
        out_specs=(VMEM, VMEM),
        scratch_shapes=[pltpu.VMEM((t, kv), F32), pltpu.VMEM((t, kv), BF16)],
        cost_estimate=pl.CostEstimate(flops=2 * t * d * kv, bytes_accessed=d * kv, transcendentals=0),
        name="far_products",
    )(at, tokens, upstream, acc, *sums, *weights)


def step(tokens, upstream, params, momentum, projection):
    rows, _ = params.shape
    n_z, n_xh, n_c = (lax.axis_size(a) for a in FSDP)
    n_isl = lax.axis_size("y") * lax.axis_size("xl")
    fsdp_count = n_z * n_xh * n_c
    width = tokens.shape[1]
    proj = projection.shape[1]
    part = rows // n_isl
    inv_width = 1.0 / math.sqrt(width)
    scale_tok = 1.0 / math.sqrt(tokens.shape[0] * fsdp_count)
    at = jnp.stack([lax.axis_index(a).astype(jnp.int32) for a in ("c", "y", "xh", "xl", "z")])
    swap = functools.partial(lax.ppermute, axis_name="c", perm=[(0, 1), (1, 0)])

    piece = make_piece(at, params, n_z, n_isl)
    other = pick(at, tokens, piece)
    got = swap(other)
    piece = lax.all_to_all(piece, "z", 0, 0, tiled=True)

    q = make_q(upstream, projection)
    got_q = swap(q)
    pair = make_sketch(at, tokens, got, q, got_q, n_z, n_xh)

    def shift(x, k):
        return lax.ppermute(x, "z", [(i, (i + k) % n_z) for i in range(n_z)])

    half_way = n_z // 2
    near_by = half_way + 1
    relayed = shift(pair[half_way], n_z - 1)
    along = pair[0].astype(F32)
    for k in range(half_way - 1, 0, -1):
        along += shift(pair[k], k).astype(F32)
        if k < half_way - 1:
            along += shift(pair[n_z - k], n_z - k).astype(F32)
    joined = (pair[near_by].astype(F32) + relayed.astype(F32)).astype(BF16)
    along += shift(joined, near_by).astype(F32)
    each = n_z // GROUPS
    held = [piece[g * each : (g + 1) * each] for g in range(GROUPS)]
    for step in range(3):
        more = [exchange(h, g, step) for g, h in enumerate(held)]
        held = [jnp.concatenate(both, axis=0) for both in zip(held, more)]
    far = [exchange(h, g, 3) for g, h in enumerate(held)]
    acc, *sums = near_products(at, tokens, upstream, [*held, *(swap(h) for h in held)])
    values, token_grads = far_products(
        at, tokens, upstream, acc, sums, [*far, *(swap(f) for f in far)], inv_width
    )

    along = along.astype(BF16)
    plane = lax.all_to_all(along.reshape(n_xh * n_isl, part, proj), PLANE, 0, 0, tiled=True)
    total = jnp.sum(plane.astype(F32), axis=0).astype(BF16)
    total = jnp.broadcast_to(total[None], (n_isl, part, proj))
    total = lax.all_to_all(total, ISLAND, 0, 0, tiled=True)
    total = total.reshape(rows, proj)

    dims = (((1,), (1,)), ((), ()))
    head, rest = two_parts(projection)
    outer = lax.dot_general(total, head, dims, preferred_element_type=F32)
    outer = outer + lax.dot_general(total, rest, dims, preferred_element_type=F32)
    outer = outer * (scale_tok / (proj * n_isl))
    new_momentum = 0.9 * momentum + outer
    new_params = params - 0.7 * (outer + 0.9 * new_momentum)

    return (values, token_grads, new_params, new_momentum)


def solution(mesh):
    fine = Mesh(mesh.devices.reshape(4, 2, 8, 2, 2), ISLAND + FSDP)
    both = ISLAND + FSDP
    in_specs = (P(both, None), P(both, None), P(FSDP, None), P(FSDP, None), P())
    out_specs = (P(both, None), P(both, None), P(FSDP, None), P(FSDP, None))
    return jax.shard_map(step, mesh=fine, in_specs=in_specs, out_specs=out_specs, check_vma=False)
```

```python
import functools
import math

import jax
import jax.numpy as jnp
from jax import lax
from jax.experimental import pallas as pl
from jax.experimental.pallas import tpu as pltpu
from jax.sharding import Mesh
from jax.sharding import PartitionSpec as P


ISLAND = ("y", "xl")
FSDP = ("z", "xh", "c")
PLANE = ("xh", "y", "xl")
F32, BF16 = jnp.float32, jnp.bfloat16
LANES = 128
VMEM = pl.BlockSpec(memory_space=pltpu.VMEM)
SMEM = pl.BlockSpec(memory_space=pltpu.SMEM)
LEFT = pl.BlockSpec(memory_space=pl.ANY)


def two_parts(x):
    head = x.astype(BF16)
    return head, (x - head.astype(F32)).astype(BF16)


def piece_kernel(at_ref, params_ref, piece_ref):
    width = piece_ref.shape[2]
    block = 2 * at_ref[1] + at_ref[3]
    piece = params_ref[:, pl.ds(pl.multiple_of(block * width, width), width)].astype(BF16)
    for z in range(piece_ref.shape[0]):
        piece_ref[z] = piece


def make_piece(at, params, n_z, pieces):
    rows, kv = params.shape
    return pl.pallas_call(
        piece_kernel,
        out_shape=jax.ShapeDtypeStruct((n_z, rows, kv // pieces), BF16),
        in_specs=[SMEM, VMEM],
        out_specs=VMEM,
        name="make_piece",
    )(at, params)


def pick_kernel(at_ref, tokens_ref, after_ref, out_ref):
    skip = 1 - at_ref[0]
    for k in range(out_ref.shape[1] // LANES):
        at = pl.multiple_of((2 * k + skip) * LANES, LANES)
        out_ref[:, k * LANES : (k + 1) * LANES] = tokens_ref[:, pl.ds(at, LANES)]


def pick(at, tokens, after):
    t, d = tokens.shape
    return pl.pallas_call(
        pick_kernel,
        out_shape=jax.ShapeDtypeStruct((t, d // 2), BF16),
        in_specs=[SMEM, VMEM, LEFT],
        out_specs=VMEM,
        name="pick",
    )(at, tokens, after)


def q_kernel(up_ref, proj_ref, q_ref):
    head, rest = two_parts(proj_ref[...])
    q = jnp.dot(up_ref[...], head, preferred_element_type=F32)
    q += jnp.dot(up_ref[...], rest, preferred_element_type=F32)
    q_ref[...] = q.astype(BF16)


def make_q(upstream, projection):
    return pl.pallas_call(
        q_kernel,
        out_shape=jax.ShapeDtypeStruct((upstream.shape[0], projection.shape[1]), BF16),
        in_specs=[VMEM, VMEM],
        out_specs=VMEM,
        cost_estimate=pl.CostEstimate(
            flops=8 * upstream.size * projection.shape[1],
            bytes_accessed=4 * projection.size + 4 * upstream.size,
            transcendentals=0,
        ),
        name="make_q",
    )(upstream, projection)


def sketch_kernel(at_ref, tok_ref, got_ref, q_ref, got_q_ref, *out_refs):
    n_z = len(out_refs)
    n_xh = out_refs[0].shape[0]
    dims = (((0,), (0,)), ((), ()))
    for r, out_ref in enumerate(out_refs):
        z = lax.rem(at_ref[4] + r, n_z)
        for h in range(n_xh):
            k = z * n_xh + h
            mine = tok_ref[:, pl.ds(pl.multiple_of((2 * k + at_ref[0]) * LANES, LANES), LANES)]
            theirs = got_ref[:, pl.ds(pl.multiple_of(k * LANES, LANES), LANES)]
            s = lax.dot_general(mine, q_ref[...], dims, preferred_element_type=F32)
            s += lax.dot_general(theirs, got_q_ref[...], dims, preferred_element_type=F32)
            out_ref[h] = s.astype(BF16)


def make_sketch(at, tokens, got, q, got_q, n_z, n_xh):
    proj = q.shape[1]
    return pl.pallas_call(
        sketch_kernel,
        out_shape=(jax.ShapeDtypeStruct((n_xh, LANES, proj), BF16),) * n_z,
        in_specs=[SMEM] + [VMEM] * 4,
        out_specs=(VMEM,) * n_z,
        cost_estimate=pl.CostEstimate(
            flops=8 * tokens.size * proj, bytes_accessed=16 * tokens.size, transcendentals=0
        ),
        name="make_sketch",
    )(at, tokens, got, q, got_q)


ORDERS = (("XALB", "LBXA"), ("ALBX", "BXAL"))
GROUPS = len(ORDERS[0])
FLIP = {"X": (1, 0, 1), "L": (0, 0, 1), "A": (0, 1, 0), "B": (0, 3, 0)}


def exchange(x, group, step):
    def index(y, xl, xh, c):
        return ((y * 2 + xl) * 2 + xh) * 2 + c

    pairs = []
    for y in range(4):
        for xl in range(2):
            for xh in range(2):
                for c in range(2):
                    a, b, l = FLIP[ORDERS[c][group][step]]
                    pairs.append((index(y, xl, xh, c), index(y ^ b, xl ^ l, xh ^ a, c)))
    return lax.ppermute(x, ("y", "xl", "xh", "c"), pairs)


def places(core, group):
    order = ORDERS[core][group]
    held = [(0, 0, 0)]
    for kind in order[:3]:
        f = FLIP[kind]
        held = held + [(a ^ f[0], b ^ f[1], l ^ f[2]) for a, b, l in held]
    f = FLIP[order[3]]
    far = [(a ^ f[0], b ^ f[1], l ^ f[2]) for a, b, l in held]
    return {
        (half, a): sorted(((b, l), i) for i, (a_, b, l) in enumerate(part) if a_ == a)
        for half, part in enumerate((held, far))
        for a in range(2)
    }


def lanes(ref, blocks):
    return jnp.concatenate([ref[:, at] for at in blocks], axis=1)


class Loads:
    def __init__(self, sources, targets, sems):
        self.targets = targets
        self.copies = [
            pltpu.make_async_copy(a, b, sems.at[i]) for i, (a, b) in enumerate(zip(sources, targets))
        ]
        for copy in self.copies:
            copy.start()
        self.left = None

    def begin(self):
        self.left = set(range(len(self.copies)))

    def get(self, i):
        if i in self.left:
            self.left.remove(i)
            self.copies[i].wait()
        return self.targets[i]

    def finish(self):
        for i in sorted(self.left):
            self.get(i)


def half_products(half, groups, core, at_ref, tok_ref, get_w, acc_ref, up_rel, take):
    xh = at_ref[2]
    each = tok_ref.shape[1] // (4 * LANES * GROUPS)
    for n, g in enumerate(groups):
        for o in range(2):
            table = places(core ^ o, g)
            w_ref = get_w(len(groups) * o + n)
            for a in range(2):
                zs = range(g * each, (g + 1) * each)
                blocks = [
                    pl.ds(pl.multiple_of((2 * (2 * z + (xh ^ a)) + (core ^ o)) * LANES, LANES), LANES) for z in zs
                ]
                found = table[half, a]
                total = None
                if found:
                    w = jnp.concatenate(
                        [
                            jnp.concatenate([w_ref[i * each + k] for _, i in found], axis=1)
                            for k in range(each)
                        ],
                        axis=0,
                    )
                    here = [slice((2 * b + l) * LANES, (2 * b + l + 1) * LANES) for (b, l), _ in found]
                    part = jnp.dot(lanes(tok_ref, blocks), w, preferred_element_type=F32)
                    for i, at in enumerate(here):
                        acc_ref[:, at] += part[:, i * LANES : (i + 1) * LANES]
                    total = lax.dot_general(
                        lanes(up_rel, here), w, (((1,), (1,)), ((), ())), preferred_element_type=F32
                    )
                take(g, a, o, blocks, total)


def columns(at_ref):
    y, xl = at_ref[1], at_ref[3]
    return [
        pl.ds(pl.multiple_of((2 * (y ^ (r // 2)) + (xl ^ (r % 2))) * LANES, LANES), LANES) for r in range(8)
    ]


def arrange(at_ref, up_ref, up_rel):
    for r, at in enumerate(columns(at_ref)):
        up_rel[:, r * LANES : (r + 1) * LANES] = up_ref[:, at]


def near_kernel(at_ref, tok_ref, up_ref, *refs):
    n = 2 * GROUPS
    w_refs, (acc_ref, *sum_refs), (up_rel, *held, sems) = refs[:n], refs[n : n + 1 + GROUPS], refs[n + 1 + GROUPS :]
    loads = Loads(w_refs, held, sems)
    acc_ref[...] = jnp.zeros(acc_ref.shape, F32)
    arrange(at_ref, up_ref, up_rel)

    def take(g, a, o, blocks, total):
        if total is not None:
            sum_refs[g][2 * a + o] = total

    for core in range(2):

        @pl.when(lax.axis_index("c") == core)
        def _():
            loads.begin()
            half_products(0, range(GROUPS), core, at_ref, tok_ref, loads.get, acc_ref, up_rel, take)
            loads.finish()


def far_kernel(at_ref, tok_ref, up_ref, before_ref, *refs, scale):
    n = 3 * GROUPS
    values_ref, grads_ref, acc_ref, up_rel, *held, sems = refs[n:]
    loads = Loads(refs[:n], held, sems)
    acc_ref[...] = before_ref[...]
    arrange(at_ref, up_ref, up_rel)

    for core in range(2):

        def take(g, a, o, blocks, total, core=core):
            if places(core ^ o, g)[0, a]:
                before = loads.get(2 * GROUPS + g)[2 * a + o]
                total = before if total is None else total + before
            grad = (total * scale).astype(BF16)
            for k, at in enumerate(blocks):
                grads_ref[:, at] = grad[:, k * LANES : (k + 1) * LANES]

        @pl.when(lax.axis_index("c") == core)
        def _():
            loads.begin()
            half_products(1, range(GROUPS), core, at_ref, tok_ref, loads.get, acc_ref, up_rel, take)
            loads.finish()

    for r, at in enumerate(columns(at_ref)):
        values_ref[:, at] = (acc_ref[:, r * LANES : (r + 1) * LANES] * scale).astype(BF16)


def loaded(arrays):
    return [*(pltpu.VMEM(a.shape, a.dtype) for a in arrays), pltpu.SemaphoreType.DMA((len(arrays),))]


def near_products(at, tokens, upstream, weights):
    t, d = tokens.shape
    kv = upstream.shape[1]
    return pl.pallas_call(
        near_kernel,
        out_shape=(
            jax.ShapeDtypeStruct((t, kv), F32),
            *[jax.ShapeDtypeStruct((4, t, d // (4 * GROUPS)), F32)] * GROUPS,
        ),
        in_specs=[SMEM, VMEM, VMEM] + [LEFT] * len(weights),
        out_specs=(VMEM,) * (1 + GROUPS),
        scratch_shapes=[pltpu.VMEM((t, kv), BF16), *loaded(weights)],
        cost_estimate=pl.CostEstimate(flops=2 * t * d * kv, bytes_accessed=d * kv, transcendentals=0),
        name="near_products",
    )(at, tokens, upstream, *weights)


def far_products(at, tokens, upstream, acc, sums, weights, scale):
    t, d = tokens.shape
    kv = upstream.shape[1]
    return pl.pallas_call(
        functools.partial(far_kernel, scale=scale),
        out_shape=(jax.ShapeDtypeStruct((t, kv), BF16), jax.ShapeDtypeStruct((t, d), BF16)),
        in_specs=[SMEM, VMEM, VMEM, VMEM] + [LEFT] * (len(sums) + len(weights)),
        out_specs=(VMEM, VMEM),
        scratch_shapes=[pltpu.VMEM((t, kv), F32), pltpu.VMEM((t, kv), BF16), *loaded([*weights, *sums])],
        cost_estimate=pl.CostEstimate(flops=2 * t * d * kv, bytes_accessed=d * kv, transcendentals=0),
        name="far_products",
    )(at, tokens, upstream, acc, *weights, *sums)


def step(tokens, upstream, params, momentum, projection):
    rows, _ = params.shape
    n_z, n_xh, n_c = (lax.axis_size(a) for a in FSDP)
    n_isl = lax.axis_size("y") * lax.axis_size("xl")
    fsdp_count = n_z * n_xh * n_c
    width = tokens.shape[1]
    proj = projection.shape[1]
    part = rows // n_isl
    inv_width = 1.0 / math.sqrt(width)
    scale_tok = 1.0 / math.sqrt(tokens.shape[0] * fsdp_count)
    at = jnp.stack([lax.axis_index(a).astype(jnp.int32) for a in ("c", "y", "xh", "xl", "z")])
    swap = functools.partial(lax.ppermute, axis_name="c", perm=[(0, 1), (1, 0)])

    piece = make_piece(at, params, n_z, n_isl)
    other = pick(at, tokens, piece)
    got = swap(other)
    piece = lax.all_to_all(piece, "z", 0, 0, tiled=True)

    q = make_q(upstream, projection)
    got_q = swap(q)
    pair = make_sketch(at, tokens, got, q, got_q, n_z, n_xh)

    def shift(x, k):
        return lax.ppermute(x, "z", [(i, (i + k) % n_z) for i in range(n_z)])

    half_way = n_z // 2
    near_by = half_way + 1
    relayed = shift(pair[half_way], n_z - 1)
    along = pair[0].astype(F32)
    for k in range(half_way - 1, 0, -1):
        along += shift(pair[k], k).astype(F32)
        if k < half_way - 1:
            along += shift(pair[n_z - k], n_z - k).astype(F32)
    joined = (pair[near_by].astype(F32) + relayed.astype(F32)).astype(BF16)
    along += shift(joined, near_by).astype(F32)
    each = n_z // GROUPS
    held = [piece[g * each : (g + 1) * each] for g in range(GROUPS)]
    for step in range(3):
        more = [exchange(h, g, step) for g, h in enumerate(held)]
        held = [jnp.concatenate(both, axis=0) for both in zip(held, more)]
    far = [exchange(h, g, 3) for g, h in enumerate(held)]
    acc, *sums = near_products(at, tokens, upstream, [*held, *(swap(h) for h in held)])
    swapped = [swap(f) for f in far]
    values, token_grads = far_products(at, tokens, upstream, acc, sums, [*far, *swapped], inv_width)

    along = along.astype(BF16)
    plane = lax.all_to_all(along.reshape(n_xh * n_isl, part, proj), PLANE, 0, 0, tiled=True)
    total = jnp.sum(plane.astype(F32), axis=0).astype(BF16)
    total = jnp.broadcast_to(total[None], (n_isl, part, proj))
    total = lax.all_to_all(total, ISLAND, 0, 0, tiled=True)
    total = total.reshape(rows, proj)

    dims = (((1,), (1,)), ((), ()))
    head, rest = two_parts(projection)
    outer = lax.dot_general(total, head, dims, preferred_element_type=F32)
    outer = outer + lax.dot_general(total, rest, dims, preferred_element_type=F32)
    outer = outer * (scale_tok / (proj * n_isl))
    new_momentum = 0.9 * momentum + outer
    new_params = params - 0.7 * (outer + 0.9 * new_momentum)

    return (values, token_grads, new_params, new_momentum)


def solution(mesh):
    fine = Mesh(mesh.devices.reshape(4, 2, 8, 2, 2), ISLAND + FSDP)
    both = ISLAND + FSDP
    in_specs = (P(both, None), P(both, None), P(FSDP, None), P(FSDP, None), P())
    out_specs = (P(both, None), P(both, None), P(FSDP, None), P(FSDP, None))
    return jax.shard_map(step, mesh=fine, in_specs=in_specs, out_specs=out_specs, check_vma=False)
```

```python
import functools
import math

import jax
import jax.numpy as jnp
from jax import lax
from jax.experimental import pallas as pl
from jax.experimental.pallas import tpu as pltpu
from jax.sharding import Mesh
from jax.sharding import PartitionSpec as P


ISLAND = ("y", "xl")
FSDP = ("z", "xh", "c")
PLANE = ("xh", "y", "xl")
F32, BF16 = jnp.float32, jnp.bfloat16
LANES = 128
VMEM = pl.BlockSpec(memory_space=pltpu.VMEM)
SMEM = pl.BlockSpec(memory_space=pltpu.SMEM)
LEFT = pl.BlockSpec(memory_space=pl.ANY)


def two_parts(x):
    head = x.astype(BF16)
    return head, (x - head.astype(F32)).astype(BF16)


def piece_kernel(at_ref, params_ref, piece_ref):
    width = piece_ref.shape[2]
    block = 2 * at_ref[1] + at_ref[3]
    piece = params_ref[:, pl.ds(pl.multiple_of(block * width, width), width)].astype(BF16)
    for z in range(piece_ref.shape[0]):
        piece_ref[z] = piece


def make_piece(at, params, n_z, pieces):
    rows, kv = params.shape
    return pl.pallas_call(
        piece_kernel,
        out_shape=jax.ShapeDtypeStruct((n_z, rows, kv // pieces), BF16),
        in_specs=[SMEM, VMEM],
        out_specs=VMEM,
        name="make_piece",
    )(at, params)


def pick_kernel(at_ref, tokens_ref, after_ref, out_ref):
    skip = 1 - at_ref[0]
    for k in range(out_ref.shape[1] // LANES):
        at = pl.multiple_of((2 * k + skip) * LANES, LANES)
        out_ref[:, k * LANES : (k + 1) * LANES] = tokens_ref[:, pl.ds(at, LANES)]


def pick(at, tokens, after):
    t, d = tokens.shape
    return pl.pallas_call(
        pick_kernel,
        out_shape=jax.ShapeDtypeStruct((t, d // 2), BF16),
        in_specs=[SMEM, VMEM, LEFT],
        out_specs=VMEM,
        name="pick",
    )(at, tokens, after)


def q_kernel(up_ref, proj_ref, q_ref):
    head, rest = two_parts(proj_ref[...])
    q = jnp.dot(up_ref[...], head, preferred_element_type=F32)
    q += jnp.dot(up_ref[...], rest, preferred_element_type=F32)
    q_ref[...] = q.astype(BF16)


def make_q(upstream, projection):
    return pl.pallas_call(
        q_kernel,
        out_shape=jax.ShapeDtypeStruct((upstream.shape[0], projection.shape[1]), BF16),
        in_specs=[VMEM, VMEM],
        out_specs=VMEM,
        cost_estimate=pl.CostEstimate(
            flops=8 * upstream.size * projection.shape[1],
            bytes_accessed=4 * projection.size + 4 * upstream.size,
            transcendentals=0,
        ),
        name="make_q",
    )(upstream, projection)


def sketch_kernel(at_ref, tok_ref, got_ref, q_ref, got_q_ref, *out_refs):
    n_z = len(out_refs)
    n_xh = out_refs[0].shape[0]
    dims = (((0,), (0,)), ((), ()))
    for r, out_ref in enumerate(out_refs):
        z = lax.rem(at_ref[4] + r, n_z)
        for h in range(n_xh):
            k = z * n_xh + h
            mine = tok_ref[:, pl.ds(pl.multiple_of((2 * k + at_ref[0]) * LANES, LANES), LANES)]
            theirs = got_ref[:, pl.ds(pl.multiple_of(k * LANES, LANES), LANES)]
            s = lax.dot_general(mine, q_ref[...], dims, preferred_element_type=F32)
            s += lax.dot_general(theirs, got_q_ref[...], dims, preferred_element_type=F32)
            out_ref[h] = s.astype(BF16)


def make_sketch(at, tokens, got, q, got_q, n_z, n_xh):
    proj = q.shape[1]
    return pl.pallas_call(
        sketch_kernel,
        out_shape=(jax.ShapeDtypeStruct((n_xh, LANES, proj), BF16),) * n_z,
        in_specs=[SMEM] + [VMEM] * 4,
        out_specs=(VMEM,) * n_z,
        cost_estimate=pl.CostEstimate(
            flops=8 * tokens.size * proj, bytes_accessed=16 * tokens.size, transcendentals=0
        ),
        name="make_sketch",
    )(at, tokens, got, q, got_q)


ORDERS = (("XALB", "LBXA"), ("ALBX", "BXAL"))
GROUPS = len(ORDERS[0])
FLIP = {"X": (1, 0, 1), "L": (0, 0, 1), "A": (0, 1, 0), "B": (0, 3, 0)}


def exchange(x, group, step):
    def index(y, xl, xh, c):
        return ((y * 2 + xl) * 2 + xh) * 2 + c

    pairs = []
    for y in range(4):
        for xl in range(2):
            for xh in range(2):
                for c in range(2):
                    a, b, l = FLIP[ORDERS[c][group][step]]
                    pairs.append((index(y, xl, xh, c), index(y ^ b, xl ^ l, xh ^ a, c)))
    return lax.ppermute(x, ("y", "xl", "xh", "c"), pairs)


def places(core, group):
    order = ORDERS[core][group]
    held = [(0, 0, 0)]
    for kind in order[:3]:
        f = FLIP[kind]
        held = held + [(a ^ f[0], b ^ f[1], l ^ f[2]) for a, b, l in held]
    f = FLIP[order[3]]
    far = [(a ^ f[0], b ^ f[1], l ^ f[2]) for a, b, l in held]
    return {
        (half, a): sorted(((b, l), i) for i, (a_, b, l) in enumerate(part) if a_ == a)
        for half, part in enumerate((held, far))
        for a in range(2)
    }


def lanes(ref, blocks):
    return jnp.concatenate([ref[:, at] for at in blocks], axis=1)


def half_products(half, groups, core, at_ref, tok_ref, w_refs, acc_ref, up_rel, take):
    xh = at_ref[2]
    each = w_refs[0].shape[0] // 8
    for n, g in enumerate(groups):
        for o in range(2):
            table = places(core ^ o, g)
            w_ref = w_refs[len(groups) * o + n]
            for a in range(2):
                zs = range(g * each, (g + 1) * each)
                blocks = [
                    pl.ds(pl.multiple_of((2 * (2 * z + (xh ^ a)) + (core ^ o)) * LANES, LANES), LANES) for z in zs
                ]
                found = table[half, a]
                total = None
                if found:
                    w = jnp.concatenate(
                        [
                            jnp.concatenate([w_ref[i * each + k] for _, i in found], axis=1)
                            for k in range(each)
                        ],
                        axis=0,
                    )
                    here = [slice((2 * b + l) * LANES, (2 * b + l + 1) * LANES) for (b, l), _ in found]
                    part = jnp.dot(lanes(tok_ref, blocks), w, preferred_element_type=F32)
                    for i, at in enumerate(here):
                        acc_ref[:, at] += part[:, i * LANES : (i + 1) * LANES]
                    total = lax.dot_general(
                        lanes(up_rel, here), w, (((1,), (1,)), ((), ())), preferred_element_type=F32
                    )
                take(g, a, o, blocks, total)


def columns(at_ref):
    y, xl = at_ref[1], at_ref[3]
    return [
        pl.ds(pl.multiple_of((2 * (y ^ (r // 2)) + (xl ^ (r % 2))) * LANES, LANES), LANES) for r in range(8)
    ]


def arrange(at_ref, up_ref, up_rel):
    for r, at in enumerate(columns(at_ref)):
        up_rel[:, r * LANES : (r + 1) * LANES] = up_ref[:, at]


def near_kernel(at_ref, tok_ref, up_ref, *refs):
    w_refs, (acc_ref, *sum_refs, up_rel) = refs[: 2 * GROUPS], refs[2 * GROUPS :]
    acc_ref[...] = jnp.zeros(acc_ref.shape, F32)
    arrange(at_ref, up_ref, up_rel)

    def take(g, a, o, blocks, total):
        if total is not None:
            sum_refs[g][2 * a + o] = total

    for core in range(2):

        @pl.when(at_ref[0] == core)
        def _():
            half_products(0, range(GROUPS), core, at_ref, tok_ref, w_refs, acc_ref, up_rel, take)


def far_kernel(at_ref, tok_ref, up_ref, before_ref, sum_ref, *refs, group, scale, last):
    w_refs = refs[:2]
    if last:
        part_ref, values_ref, grads_ref, acc_ref, up_rel = refs[2:]
        done = part_ref.shape[1]
        grads_ref[:, :done] = part_ref[...]
    else:
        acc_ref, grads_ref, up_rel = refs[2:]
    acc_ref[...] = before_ref[...]
    arrange(at_ref, up_ref, up_rel)

    for core in range(2):

        def take(g, a, o, blocks, total, core=core):
            if places(core ^ o, g)[0, a]:
                before = sum_ref[2 * a + o]
                total = before if total is None else total + before
            grad = (total * scale).astype(BF16)
            for k, at in enumerate(blocks):
                grads_ref[:, at] = grad[:, k * LANES : (k + 1) * LANES]

        @pl.when(at_ref[0] == core)
        def _():
            half_products(1, (group,), core, at_ref, tok_ref, w_refs, acc_ref, up_rel, take)

    if last:
        for r, at in enumerate(columns(at_ref)):
            values_ref[:, at] = (acc_ref[:, r * LANES : (r + 1) * LANES] * scale).astype(BF16)


def near_products(at, tokens, upstream, weights):
    t, d = tokens.shape
    kv = upstream.shape[1]
    return pl.pallas_call(
        near_kernel,
        out_shape=(
            jax.ShapeDtypeStruct((t, kv), F32),
            *[jax.ShapeDtypeStruct((4, t, d // (4 * GROUPS)), F32)] * GROUPS,
        ),
        in_specs=[SMEM] + [VMEM] * (2 + len(weights)),
        out_specs=(VMEM,) * (1 + GROUPS),
        scratch_shapes=[pltpu.VMEM((t, kv), BF16)],
        cost_estimate=pl.CostEstimate(flops=2 * t * d * kv, bytes_accessed=d * kv, transcendentals=0),
        name="near_products",
    )(at, tokens, upstream, *weights)


def far_products(at, tokens, upstream, acc, sums, weights, scale, group, part=None):
    t, d = tokens.shape
    kv = upstream.shape[1]
    last = part is not None
    rel = pltpu.VMEM((t, kv), BF16)
    if last:
        shapes = (jax.ShapeDtypeStruct((t, kv), BF16), jax.ShapeDtypeStruct((t, d), BF16))
        extra, scratch = (part,), [pltpu.VMEM((t, kv), F32), rel]
    else:
        shapes = (jax.ShapeDtypeStruct((t, kv), F32), jax.ShapeDtypeStruct((t, d // GROUPS), BF16))
        extra, scratch = (), [rel]
    return pl.pallas_call(
        functools.partial(far_kernel, group=group, scale=scale, last=last),
        out_shape=shapes,
        in_specs=[SMEM] + [VMEM] * (6 + len(extra)),
        out_specs=(VMEM, VMEM),
        scratch_shapes=scratch,
        cost_estimate=pl.CostEstimate(flops=t * d * kv, bytes_accessed=d * kv, transcendentals=0),
        name="far_products",
    )(at, tokens, upstream, acc, sums, *weights, *extra)


def step(tokens, upstream, params, momentum, projection):
    rows, _ = params.shape
    n_z, n_xh, n_c = (lax.axis_size(a) for a in FSDP)
    n_isl = lax.axis_size("y") * lax.axis_size("xl")
    fsdp_count = n_z * n_xh * n_c
    width = tokens.shape[1]
    proj = projection.shape[1]
    part = rows // n_isl
    inv_width = 1.0 / math.sqrt(width)
    scale_tok = 1.0 / math.sqrt(tokens.shape[0] * fsdp_count)
    at = jnp.stack([lax.axis_index(a).astype(jnp.int32) for a in ("c", "y", "xh", "xl", "z")])
    swap = functools.partial(lax.ppermute, axis_name="c", perm=[(0, 1), (1, 0)])

    piece = make_piece(at, params, n_z, n_isl)
    other = pick(at, tokens, piece)
    got = swap(other)
    piece = lax.all_to_all(piece, "z", 0, 0, tiled=True)

    q = make_q(upstream, projection)
    got_q = swap(q)
    pair = make_sketch(at, tokens, got, q, got_q, n_z, n_xh)

    def shift(x, k):
        return lax.ppermute(x, "z", [(i, (i + k) % n_z) for i in range(n_z)])

    half_way = n_z // 2
    near_by = half_way + 1
    relayed = shift(pair[half_way], n_z - 1)
    along = pair[0].astype(F32)
    for k in range(half_way - 1, 0, -1):
        along += shift(pair[k], k).astype(F32)
        if k < half_way - 1:
            along += shift(pair[n_z - k], n_z - k).astype(F32)
    joined = (pair[near_by].astype(F32) + relayed.astype(F32)).astype(BF16)
    along += shift(joined, near_by).astype(F32)
    each = n_z // GROUPS
    held = [piece[g * each : (g + 1) * each] for g in range(GROUPS)]
    for step in range(3):
        more = [exchange(h, g, step) for g, h in enumerate(held)]
        held = [jnp.concatenate(both, axis=0) for both in zip(held, more)]
    far = [exchange(h, g, 3) for g, h in enumerate(held)]
    acc, *sums = near_products(at, tokens, upstream, [*held, *(swap(h) for h in held)])
    far = [(f, swap(f)) for f in far]
    acc, grads = far_products(at, tokens, upstream, acc, sums[0], far[0], inv_width, 0)
    values, token_grads = far_products(
        at, tokens, upstream, acc, sums[1], far[1], inv_width, 1, grads
    )

    along = along.astype(BF16)
    plane = lax.all_to_all(along.reshape(n_xh * n_isl, part, proj), PLANE, 0, 0, tiled=True)
    total = jnp.sum(plane.astype(F32), axis=0).astype(BF16)
    total = jnp.broadcast_to(total[None], (n_isl, part, proj))
    total = lax.all_to_all(total, ISLAND, 0, 0, tiled=True)
    total = total.reshape(rows, proj)

    dims = (((1,), (1,)), ((), ()))
    head, rest = two_parts(projection)
    outer = lax.dot_general(total, head, dims, preferred_element_type=F32)
    outer = outer + lax.dot_general(total, rest, dims, preferred_element_type=F32)
    outer = outer * (scale_tok / (proj * n_isl))
    new_momentum = 0.9 * momentum + outer
    new_params = params - 0.7 * (outer + 0.9 * new_momentum)

    return (values, token_grads, new_params, new_momentum)


def solution(mesh):
    fine = Mesh(mesh.devices.reshape(4, 2, 8, 2, 2), ISLAND + FSDP)
    both = ISLAND + FSDP
    in_specs = (P(both, None), P(both, None), P(FSDP, None), P(FSDP, None), P())
    out_specs = (P(both, None), P(both, None), P(FSDP, None), P(FSDP, None))
    return jax.shard_map(step, mesh=fine, in_specs=in_specs, out_specs=out_specs, check_vma=False)
```

```python
import functools
import math

import jax
import jax.numpy as jnp
from jax import lax
from jax.experimental import pallas as pl
from jax.experimental.pallas import tpu as pltpu
from jax.sharding import Mesh
from jax.sharding import PartitionSpec as P


ISLAND = ("y", "xl")
FSDP = ("z", "xh", "c")
PLANE = ("xh", "y", "xl")
F32, BF16 = jnp.float32, jnp.bfloat16
LANES = 128
VMEM = pl.BlockSpec(memory_space=pltpu.VMEM)
SMEM = pl.BlockSpec(memory_space=pltpu.SMEM)
LEFT = pl.BlockSpec(memory_space=pl.ANY)


def piece_kernel(at_ref, params_ref, piece_ref):
    width = piece_ref.shape[2]
    block = 2 * at_ref[1] + at_ref[3]
    piece = params_ref[:, pl.ds(pl.multiple_of(block * width, width), width)].astype(BF16)
    for z in range(piece_ref.shape[0]):
        piece_ref[z] = piece


def make_piece(at, params, n_z, pieces):
    rows, kv = params.shape
    return pl.pallas_call(
        piece_kernel,
        out_shape=jax.ShapeDtypeStruct((n_z, rows, kv // pieces), BF16),
        in_specs=[SMEM, VMEM],
        out_specs=VMEM,
        name="make_piece",
    )(at, params)


def pick_kernel(at_ref, tokens_ref, after_ref, out_ref):
    skip = 1 - at_ref[0]
    for k in range(out_ref.shape[1] // LANES):
        at = pl.multiple_of((2 * k + skip) * LANES, LANES)
        out_ref[:, k * LANES : (k + 1) * LANES] = tokens_ref[:, pl.ds(at, LANES)]


def pick(at, tokens, after):
    t, d = tokens.shape
    return pl.pallas_call(
        pick_kernel,
        out_shape=jax.ShapeDtypeStruct((t, d // 2), BF16),
        in_specs=[SMEM, VMEM, LEFT],
        out_specs=VMEM,
        name="pick",
    )(at, tokens, after)


def q_kernel(up_ref, proj_ref, q_ref):
    q = jnp.dot(up_ref[...], proj_ref[...].astype(BF16), preferred_element_type=F32)
    q_ref[...] = q.astype(BF16)


def make_q(upstream, projection):
    return pl.pallas_call(
        q_kernel,
        out_shape=jax.ShapeDtypeStruct((upstream.shape[0], projection.shape[1]), BF16),
        in_specs=[VMEM, VMEM],
        out_specs=VMEM,
        cost_estimate=pl.CostEstimate(
            flops=8 * upstream.size * projection.shape[1],
            bytes_accessed=4 * projection.size + 4 * upstream.size,
            transcendentals=0,
        ),
        name="make_q",
    )(upstream, projection)


def sketch_kernel(at_ref, tok_ref, got_ref, q_ref, got_q_ref, *out_refs):
    n_z = len(out_refs)
    n_xh = out_refs[0].shape[0]
    dims = (((0,), (0,)), ((), ()))
    for r, out_ref in enumerate(out_refs):
        z = lax.rem(at_ref[4] + r, n_z)
        for h in range(n_xh):
            k = z * n_xh + h
            mine = tok_ref[:, pl.ds(pl.multiple_of((2 * k + at_ref[0]) * LANES, LANES), LANES)]
            theirs = got_ref[:, pl.ds(pl.multiple_of(k * LANES, LANES), LANES)]
            s = lax.dot_general(mine, q_ref[...], dims, preferred_element_type=F32)
            s += lax.dot_general(theirs, got_q_ref[...], dims, preferred_element_type=F32)
            out_ref[h] = s.astype(BF16)


def make_sketch(at, tokens, got, q, got_q, n_z, n_xh):
    proj = q.shape[1]
    return pl.pallas_call(
        sketch_kernel,
        out_shape=(jax.ShapeDtypeStruct((n_xh, LANES, proj), BF16),) * n_z,
        in_specs=[SMEM] + [VMEM] * 4,
        out_specs=(VMEM,) * n_z,
        cost_estimate=pl.CostEstimate(
            flops=8 * tokens.size * proj, bytes_accessed=16 * tokens.size, transcendentals=0
        ),
        name="make_sketch",
    )(at, tokens, got, q, got_q)


ORDERS = (("XALB", "LBXA"), ("ALBX", "BXAL"))
GROUPS = len(ORDERS[0])
FLIP = {"X": (1, 0, 1), "L": (0, 0, 1), "A": (0, 1, 0), "B": (0, 3, 0)}


def exchange(x, group, step):
    def index(y, xl, xh, c):
        return ((y * 2 + xl) * 2 + xh) * 2 + c

    pairs = []
    for y in range(4):
        for xl in range(2):
            for xh in range(2):
                for c in range(2):
                    a, b, l = FLIP[ORDERS[c][group][step]]
                    pairs.append((index(y, xl, xh, c), index(y ^ b, xl ^ l, xh ^ a, c)))
    return lax.ppermute(x, ("y", "xl", "xh", "c"), pairs)


def places(core, group):
    order = ORDERS[core][group]
    held = [(0, 0, 0)]
    for kind in order[:3]:
        f = FLIP[kind]
        held = held + [(a ^ f[0], b ^ f[1], l ^ f[2]) for a, b, l in held]
    f = FLIP[order[3]]
    far = [(a ^ f[0], b ^ f[1], l ^ f[2]) for a, b, l in held]
    return {
        (half, a): sorted(((b, l), i) for i, (a_, b, l) in enumerate(part) if a_ == a)
        for half, part in enumerate((held, far))
        for a in range(2)
    }


def lanes(ref, blocks):
    return jnp.concatenate([ref[:, at] for at in blocks], axis=1)


def half_products(half, groups, core, at_ref, tok_ref, w_refs, acc_ref, up_rel, take):
    xh = at_ref[2]
    each = w_refs[0].shape[0] // 8
    for n, g in enumerate(groups):
        for o in range(2):
            table = places(core ^ o, g)
            w_ref = w_refs[len(groups) * o + n]
            for a in range(2):
                zs = range(g * each, (g + 1) * each)
                blocks = [
                    pl.ds(pl.multiple_of((2 * (2 * z + (xh ^ a)) + (core ^ o)) * LANES, LANES), LANES) for z in zs
                ]
                found = table[half, a]
                total = None
                if found:
                    w = jnp.concatenate(
                        [
                            jnp.concatenate([w_ref[i * each + k] for _, i in found], axis=1)
                            for k in range(each)
                        ],
                        axis=0,
                    )
                    here = [slice((2 * b + l) * LANES, (2 * b + l + 1) * LANES) for (b, l), _ in found]
                    part = jnp.dot(lanes(tok_ref, blocks), w, preferred_element_type=F32)
                    for i, at in enumerate(here):
                        acc_ref[:, at] += part[:, i * LANES : (i + 1) * LANES]
                    total = lax.dot_general(
                        lanes(up_rel, here), w, (((1,), (1,)), ((), ())), preferred_element_type=F32
                    )
                take(g, a, o, blocks, total)


def columns(at_ref):
    y, xl = at_ref[1], at_ref[3]
    return [
        pl.ds(pl.multiple_of((2 * (y ^ (r // 2)) + (xl ^ (r % 2))) * LANES, LANES), LANES) for r in range(8)
    ]


def arrange(at_ref, up_ref, up_rel):
    for r, at in enumerate(columns(at_ref)):
        up_rel[:, r * LANES : (r + 1) * LANES] = up_ref[:, at]


def near_kernel(at_ref, tok_ref, up_ref, *refs):
    w_refs, (acc_ref, *sum_refs, up_rel) = refs[: 2 * GROUPS], refs[2 * GROUPS :]
    acc_ref[...] = jnp.zeros(acc_ref.shape, F32)
    arrange(at_ref, up_ref, up_rel)

    def take(g, a, o, blocks, total):
        if total is not None:
            sum_refs[g][2 * a + o] = total

    for core in range(2):

        @pl.when(at_ref[0] == core)
        def _():
            half_products(0, range(GROUPS), core, at_ref, tok_ref, w_refs, acc_ref, up_rel, take)


def far_kernel(at_ref, tok_ref, up_ref, before_ref, *refs, scale):
    sum_refs, w_refs = refs[:GROUPS], refs[GROUPS : 3 * GROUPS]
    values_ref, grads_ref, acc_ref, up_rel = refs[3 * GROUPS :]
    acc_ref[...] = before_ref[...]
    arrange(at_ref, up_ref, up_rel)

    for core in range(2):

        def take(g, a, o, blocks, total, core=core):
            if places(core ^ o, g)[0, a]:
                before = sum_refs[g][2 * a + o]
                total = before if total is None else total + before
            grad = (total * scale).astype(BF16)
            for k, at in enumerate(blocks):
                grads_ref[:, at] = grad[:, k * LANES : (k + 1) * LANES]

        @pl.when(at_ref[0] == core)
        def _():
            half_products(1, range(GROUPS), core, at_ref, tok_ref, w_refs, acc_ref, up_rel, take)

    for r, at in enumerate(columns(at_ref)):
        values_ref[:, at] = (acc_ref[:, r * LANES : (r + 1) * LANES] * scale).astype(BF16)


def near_products(at, tokens, upstream, weights):
    t, d = tokens.shape
    kv = upstream.shape[1]
    return pl.pallas_call(
        near_kernel,
        out_shape=(
            jax.ShapeDtypeStruct((t, kv), F32),
            *[jax.ShapeDtypeStruct((4, t, d // (4 * GROUPS)), F32)] * GROUPS,
        ),
        in_specs=[SMEM] + [VMEM] * (2 + len(weights)),
        out_specs=(VMEM,) * (1 + GROUPS),
        scratch_shapes=[pltpu.VMEM((t, kv), BF16)],
        cost_estimate=pl.CostEstimate(flops=2 * t * d * kv, bytes_accessed=d * kv, transcendentals=0),
        name="near_products",
    )(at, tokens, upstream, *weights)


def far_products(at, tokens, upstream, acc, sums, weights, scale):
    t, d = tokens.shape
    kv = upstream.shape[1]
    return pl.pallas_call(
        functools.partial(far_kernel, scale=scale),
        out_shape=(jax.ShapeDtypeStruct((t, kv), BF16), jax.ShapeDtypeStruct((t, d), BF16)),
        in_specs=[SMEM] + [VMEM] * (3 + len(sums) + len(weights)),
        out_specs=(VMEM, VMEM),
        scratch_shapes=[pltpu.VMEM((t, kv), F32), pltpu.VMEM((t, kv), BF16)],
        cost_estimate=pl.CostEstimate(flops=2 * t * d * kv, bytes_accessed=d * kv, transcendentals=0),
        name="far_products",
    )(at, tokens, upstream, acc, *sums, *weights)


def step(tokens, upstream, params, momentum, projection):
    rows, _ = params.shape
    n_z, n_xh, n_c = (lax.axis_size(a) for a in FSDP)
    n_isl = lax.axis_size("y") * lax.axis_size("xl")
    fsdp_count = n_z * n_xh * n_c
    width = tokens.shape[1]
    proj = projection.shape[1]
    part = rows // n_isl
    inv_width = 1.0 / math.sqrt(width)
    scale_tok = 1.0 / math.sqrt(tokens.shape[0] * fsdp_count)
    at = jnp.stack([lax.axis_index(a).astype(jnp.int32) for a in ("c", "y", "xh", "xl", "z")])
    swap = functools.partial(lax.ppermute, axis_name="c", perm=[(0, 1), (1, 0)])

    piece = make_piece(at, params, n_z, n_isl)
    other = pick(at, tokens, piece)
    got = swap(other)
    piece = lax.all_to_all(piece, "z", 0, 0, tiled=True)

    q = make_q(upstream, projection)
    got_q = swap(q)
    pair = make_sketch(at, tokens, got, q, got_q, n_z, n_xh)

    def shift(x, k):
        return lax.ppermute(x, "z", [(i, (i + k) % n_z) for i in range(n_z)])

    half_way = n_z // 2
    near_by = half_way + 1
    relayed = shift(pair[half_way], n_z - 1)
    along = pair[0].astype(F32)
    for k in range(half_way - 1, 0, -1):
        along += shift(pair[k], k).astype(F32)
        if k < half_way - 1:
            along += shift(pair[n_z - k], n_z - k).astype(F32)
    joined = (pair[near_by].astype(F32) + relayed.astype(F32)).astype(BF16)
    along += shift(joined, near_by).astype(F32)
    each = n_z // GROUPS
    held = [piece[g * each : (g + 1) * each] for g in range(GROUPS)]
    for step in range(3):
        more = [exchange(h, g, step) for g, h in enumerate(held)]
        held = [jnp.concatenate(both, axis=0) for both in zip(held, more)]
    far = [exchange(h, g, 3) for g, h in enumerate(held)]
    acc, *sums = near_products(at, tokens, upstream, [*held, *(swap(h) for h in held)])
    swapped = [swap(f) for f in far]
    values, token_grads = far_products(at, tokens, upstream, acc, sums, [*far, *swapped], inv_width)

    along = along.astype(BF16)
    plane = lax.all_to_all(along.reshape(n_xh * n_isl, part, proj), PLANE, 0, 0, tiled=True)
    total = jnp.sum(plane.astype(F32), axis=0).astype(BF16)
    total = jnp.broadcast_to(total[None], (n_isl, part, proj))
    total = lax.all_to_all(total, ISLAND, 0, 0, tiled=True)
    total = total.reshape(rows, proj)

    dims = (((1,), (1,)), ((), ()))
    outer = lax.dot_general(total, projection.astype(BF16), dims, preferred_element_type=F32)
    outer = outer * (scale_tok / (proj * n_isl))
    new_momentum = 0.9 * momentum + outer
    new_params = params - 0.7 * (outer + 0.9 * new_momentum)

    return (values, token_grads, new_params, new_momentum)


def solution(mesh):
    fine = Mesh(mesh.devices.reshape(4, 2, 8, 2, 2), ISLAND + FSDP)
    both = ISLAND + FSDP
    in_specs = (P(both, None), P(both, None), P(FSDP, None), P(FSDP, None), P())
    out_specs = (P(both, None), P(both, None), P(FSDP, None), P(FSDP, None))
    return jax.shard_map(step, mesh=fine, in_specs=in_specs, out_specs=out_specs, check_vma=False)
```
